256 devices in a mesh: dp: 8 (over x, core), expert: 32 (over z, y).
Axes of the slice: x: 4, y: 4, z: 8, core: 2. Of those that a mesh axis runs over, the one named last changes fastest.
Arguments:
- tokens: bfloat16 [32768, 1024], P(('dp', 'expert')), may hold values from -6 to 6
- router: float32 [1024, 32], replicated, may hold values from -0.1875 to 0.1875
- expert_lists: int32 [32768, 4], P(('dp', 'expert')), may hold values from 0 to 31, as said below
- slot_positions: int32 [32768, 4], P(('dp', 'expert')), may hold values from 0 to 19, as said below
- teacher_gate: bfloat16 [1024, 2752], P(None, 'expert'), may hold values from -0.1875 to 0.1875
- teacher_up: bfloat16 [1024, 2752], P(None, 'expert'), may hold values from -0.1875 to 0.1875
- teacher_down: bfloat16 [2752, 1024], P('expert'), may hold values from -0.109375 to 0.109375
- expert_gate: bfloat16 [32, 1024, 704], P('expert'), may hold values from -0.1875 to 0.1875
- expert_up: bfloat16 [32, 1024, 704], P('expert'), may hold values from -0.1875 to 0.1875
- expert_down: bfloat16 [32, 704, 1024], P('expert'), may hold values from -0.21875 to 0.21875
Outputs:
- grad_gate: float32 [32, 1024, 704], P('expert', 'dp')
- grad_up: float32 [32, 1024, 704], P('expert', 'dp')
- grad_down: float32 [32, 704, 1024], P('expert', None, 'dp')
The draws below stay inside these ranges and needn't reach their ends.
Inputs may be any that keep to these rules, and one draw needn't show every extreme that they name: `expert_lists`: the k-th expert of every token lies among k * 8 to (k + 1) * 8 - 1. The tokens of one device name each expert at most 20 times. For each index of dp and each such quarter of the experts, one expert is named exactly 20 times by the tokens of every device of that index. `slot_positions`: copies from the tokens of one device that name the same expert have distinct slots.
All inputs are finite; a program needn't handle non-finite values.
Results may differ from the reference program's by a relative error of at most 0.015.
Values may be sent and summed in bfloat16 or wider, within the bound.
No kernel may reach another device: no remote copies, remote signals or barrier semaphores. Data moves between devices by JAX's collectives and lax.ppermute only.
A program may use at most 128 MiB of HBM per device.

```python
import math
import jax
import jax.numpy as jnp
from jax import lax

D = 1024
EFF = 704
TFF = 2752
TOPK = 4
TOK_DEV = 128
EXPERTS = 32
CAP = 20
TOKENS = 32768
ROWS = 4096
N_DP = 8
N_EXPERT = 32


def route_tables(key):
    blocks = TOKENS // TOK_DEV
    quarter = EXPERTS // TOPK
    others = max(quarter - 1, 1)
    remain = TOK_DEV - CAP
    half_step = max(min(remain // (2 * others), (CAP - remain // others - 2) // 2), 0)
    hot_table = jax.random.randint(jax.random.fold_in(key, 7101), (N_DP, TOPK), 0, quarter)

    def one_column(block_index, column):
        column_key = jax.random.fold_in(jax.random.fold_in(key, 7202), block_index * TOPK + column)
        keys_three = jax.random.split(column_key, 3)
        order = jax.random.permutation(keys_three[0], TOK_DEV).astype(jnp.int32)
        inner = jnp.arange(1, others, dtype=jnp.int32)
        jitter = jax.random.randint(keys_three[1], (others - 1,), -half_step, half_step + 1)
        cuts = inner * remain // others + jitter
        rest = order - CAP
        label_rest = 1 + jnp.sum((rest[:, None] >= cuts[None, :]).astype(jnp.int32), axis=1)
        starts = jnp.concatenate([jnp.zeros((1,), jnp.int32), cuts.astype(jnp.int32)])
        rank_rest = rest - starts[label_rest - 1]
        is_hot = order < CAP
        label = jnp.where(is_hot, 0, label_rest)
        rank = jnp.where(is_hot, order, rank_rest)
        hot_here = hot_table[block_index // N_EXPERT, column]
        within = (label + hot_here) % quarter
        expert_id = column * quarter + within
        shifts = jax.random.randint(keys_three[2], (quarter,), 0, CAP)
        slot_id = (rank + shifts[within]) % CAP
        return (expert_id.astype(jnp.int32), slot_id.astype(jnp.int32))
    inner_map = jax.vmap(one_column, in_axes=(None, 0))
    outer_map = jax.vmap(inner_map, in_axes=(0, None))
    expert_ids, slot_ids = outer_map(jnp.arange(blocks, dtype=jnp.int32), jnp.arange(TOPK, dtype=jnp.int32))
    expert_ids = jnp.transpose(expert_ids, (0, 2, 1)).reshape(TOKENS, TOPK)
    slot_ids = jnp.transpose(slot_ids, (0, 2, 1)).reshape(TOKENS, TOPK)
    return (expert_ids, slot_ids)


def draw_expert_lists(key, part):
    return route_tables(key)[0]


def draw_slot_positions(key, part):
    return route_tables(key)[1]


def level_of(rng, extent, cuts, least, top_value):
    gain = 1.0
    for axis_at, blocks in cuts:
        heights = jax.random.uniform(jax.random.fold_in(jax.random.fold_in(rng, 6), axis_at), (blocks,), jnp.float32, least / len(cuts), top_value / len(cuts))
        gain = gain * jnp.repeat(jnp.exp(heights), extent[axis_at] // blocks).reshape((-1,) + (1,) * (len(extent) - 1 - axis_at))
    return gain


def centred(rng, dims, spread, reach, cuts=(), kind=jnp.bfloat16):
    array = spread * jax.random.normal(rng, dims, jnp.float32)
    if cuts:
        array = array * level_of(rng, dims, cuts, -0.22, 0.18)
    return jnp.clip(array, -reach, reach).astype(kind)


def setup_inputs(seed: int = 0) -> dict:
    seeds = jax.random.split(jax.random.key(seed), 11)
    tokens = centred(seeds[0], (TOKENS, D), 1.0, 6.0, ((0, 256),))
    router = centred(seeds[1], (D, EXPERTS), D ** -0.5, 0.1875, (), jnp.float32)
    expert_lists = draw_expert_lists(jax.random.fold_in(seeds[10], 71), 0)
    slot_positions = draw_slot_positions(jax.random.fold_in(seeds[10], 71), 0)
    teacher_gate = centred(seeds[4], (D, TFF), D ** -0.5, 0.1875, ((1, 32),))
    teacher_up = centred(seeds[5], (D, TFF), D ** -0.5, 0.1875, ((1, 32),))
    teacher_down = centred(seeds[6], (TFF, D), TFF ** -0.5, 0.109375, ((0, 32),))
    expert_gate = centred(seeds[7], (EXPERTS, D, EFF), D ** -0.5, 0.1875, ((0, 32),))
    expert_up = centred(seeds[8], (EXPERTS, D, EFF), D ** -0.5, 0.1875, ((0, 32),))
    expert_down = centred(seeds[9], (EXPERTS, EFF, D), EFF ** -0.5, 0.21875, ((0, 32),))
    return dict(tokens=tokens, router=router, expert_lists=expert_lists, slot_positions=slot_positions, teacher_gate=teacher_gate, teacher_up=teacher_up, teacher_down=teacher_down, expert_gate=expert_gate, expert_up=expert_up, expert_down=expert_down)


def silu_value(values):
    return values * jax.nn.sigmoid(values)

def reference(tokens, router, expert_lists, slot_positions, teacher_gate, teacher_up, teacher_down, expert_gate, expert_up, expert_down):
    shard_width = TFF // N_EXPERT

    def teacher_step(running, block_index):
        first_unit = (block_index * shard_width).astype(jnp.int32)
        gate_block = lax.dynamic_slice_in_dim(teacher_gate, first_unit, shard_width, 1)
        up_block = lax.dynamic_slice_in_dim(teacher_up, first_unit, shard_width, 1)
        down_block = lax.dynamic_slice_in_dim(teacher_down, first_unit, shard_width, 0)
        pre_a = jnp.dot(tokens, gate_block, preferred_element_type=jnp.float32)
        pre_b = jnp.dot(tokens, up_block, preferred_element_type=jnp.float32)
        hidden_block = (silu_value(pre_a) * pre_b).astype(jnp.bfloat16)
        partial_out = jnp.dot(hidden_block, down_block, preferred_element_type=jnp.float32).astype(jnp.bfloat16)
        partial_out = lax.optimization_barrier(partial_out)
        return (running + partial_out.astype(jnp.float32), None)
    teacher_total, unused = lax.scan(teacher_step, jnp.zeros((TOKENS, D), jnp.float32), jnp.arange(N_EXPERT, dtype=jnp.int32))
    target = teacher_total.astype(jnp.bfloat16)
    logits = jnp.dot(tokens.astype(jnp.float32), router, precision=lax.Precision.HIGHEST)
    picked = jnp.take_along_axis(logits, expert_lists, axis=1)
    sigmoid_pick = jax.nn.sigmoid(picked)
    weights = sigmoid_pick / lax.optimization_barrier(jnp.sum(sigmoid_pick, axis=1, keepdims=True))
    loss_scale = TOPK / math.sqrt(ROWS)
    group_size = TOK_DEV * N_EXPERT
    buffer_rows = N_EXPERT * CAP
    highest = lax.Precision.HIGHEST

    def group_step(carry, group_index):
        first_row = (group_index * group_size).astype(jnp.int32)
        group_tokens = lax.dynamic_slice_in_dim(tokens, first_row, group_size, 0)
        group_lists = lax.dynamic_slice_in_dim(expert_lists, first_row, group_size, 0)
        group_slots = lax.dynamic_slice_in_dim(slot_positions, first_row, group_size, 0)
        group_weights = lax.dynamic_slice_in_dim(weights, first_row, group_size, 0)
        group_target = lax.dynamic_slice_in_dim(target, first_row, group_size, 0)
        source = (jnp.arange(group_size, dtype=jnp.int32) // TOK_DEV)[:, None]
        flat_index = group_lists * buffer_rows + source * CAP + group_slots
        owner_index = jnp.zeros((EXPERTS * buffer_rows,), jnp.int32).at[flat_index.reshape(-1)].set(jnp.repeat(jnp.arange(group_size, dtype=jnp.int32) + 1, TOPK))
        filled = owner_index > 0
        expert_rows = jnp.where(filled[:, None], group_tokens[jnp.maximum(owner_index - 1, 0)], jnp.zeros((), jnp.bfloat16)).reshape(EXPERTS, buffer_rows, D)
        rows_wide = expert_rows.astype(jnp.float32)
        pre_gate = jnp.einsum('end,edf->enf', rows_wide, expert_gate.astype(jnp.float32), precision=highest)
        pre_up = jnp.einsum('end,edf->enf', rows_wide, expert_up.astype(jnp.float32), precision=highest)
        hidden = (silu_value(pre_gate) * pre_up).astype(jnp.bfloat16)
        down_wide = expert_down.astype(jnp.float32)
        expert_out = jnp.einsum('enf,efd->end', hidden.astype(jnp.float32), down_wide, precision=highest).astype(jnp.bfloat16)
        copies = expert_out.reshape(EXPERTS * buffer_rows, D)[flat_index]
        student = lax.optimization_barrier(jnp.sum(group_weights[:, :, None] * copies.astype(jnp.float32), axis=1))
        scaled_error = (student - group_target.astype(jnp.float32)) * loss_scale
        cotangent = (group_weights[:, :, None] * scaled_error[:, None, :]).astype(jnp.bfloat16)
        cot_buffer = jnp.zeros((EXPERTS * buffer_rows, D), jnp.bfloat16).at[flat_index.reshape(-1)].set(cotangent.reshape(-1, D)).reshape(EXPERTS, buffer_rows, D)
        cot_wide = cot_buffer.astype(jnp.float32)
        grad_hidden = jnp.einsum('end,efd->enf', cot_wide, down_wide, precision=highest)
        gate_sigmoid = jax.nn.sigmoid(pre_gate)
        grad_pre_gate = (grad_hidden * pre_up * gate_sigmoid * (1.0 + pre_gate * (1.0 - gate_sigmoid))).astype(jnp.bfloat16)
        grad_pre_up = (grad_hidden * (pre_gate * gate_sigmoid)).astype(jnp.bfloat16)
        part_gate = jnp.einsum('end,enf->edf', rows_wide, grad_pre_gate.astype(jnp.float32), precision=highest).astype(jnp.bfloat16)
        part_up = jnp.einsum('end,enf->edf', rows_wide, grad_pre_up.astype(jnp.float32), precision=highest).astype(jnp.bfloat16)
        part_down = jnp.einsum('enf,end->efd', hidden.astype(jnp.float32), cot_wide, precision=highest).astype(jnp.bfloat16)
        part_gate, part_up, part_down = lax.optimization_barrier((part_gate, part_up, part_down))
        sum_gate, sum_up, sum_down = carry
        return ((sum_gate + part_gate.astype(jnp.float32), sum_up + part_up.astype(jnp.float32), sum_down + part_down.astype(jnp.float32)), None)
    start_carry = (jnp.zeros((EXPERTS, D, EFF), jnp.float32), jnp.zeros((EXPERTS, D, EFF), jnp.float32), jnp.zeros((EXPERTS, EFF, D), jnp.float32))
    sums, unused_too = lax.scan(group_step, start_carry, jnp.arange(N_DP, dtype=jnp.int32))
    return (sums[0], sums[1], sums[2])
```

```python
import functools
import math

import jax
import jax.numpy as jnp
from jax import lax
from jax.experimental import pallas as pl
from jax.experimental.pallas import tpu as pltpu
from jax.sharding import Mesh, PartitionSpec as P

BF16 = jnp.bfloat16
F32 = jnp.float32
ALL = ("x", "core", "zq", "zp", "y")
DP = ("x", "core")
EXPERT = ("zq", "zp", "y")
QUARTER = ("zp", "y")
VMEM = pl.BlockSpec(memory_space=pltpu.VMEM)
SMEM = pl.BlockSpec(memory_space=pltpu.SMEM)
STEP = 24


def call(body, outs, args, specs=None, scratch=(), flops=0, name=None):
    moved = sum(a.size * a.dtype.itemsize for a in args)
    moved += sum(math.prod(o.shape) * o.dtype.itemsize for o in outs)
    result = pl.pallas_call(
        body,
        out_shape=tuple(outs),
        in_specs=specs or [VMEM] * len(args),
        out_specs=tuple([VMEM] * len(outs)),
        scratch_shapes=list(scratch),
        cost_estimate=pl.CostEstimate(flops=flops, bytes_accessed=moved, transcendentals=0),
        compiler_params=pltpu.CompilerParams(vmem_limit_bytes=56 * 1024 * 1024),
        name=name,
    )(*args)
    return result


def shape(dims, dtype):
    return jax.ShapeDtypeStruct(dims, dtype)


def nt(a, b):
    return lax.dot_general(a, b, (((1,), (1,)), ((), ())), preferred_element_type=F32)


def tn(a, b):
    return lax.dot_general(a, b, (((0,), (0,)), ((), ())), preferred_element_type=F32)


def nn(a, b):
    return jnp.dot(a, b, preferred_element_type=F32)


def sigmoid(v):
    return 1.0 / (1.0 + jnp.exp(-v))


def split(v):
    high = v.astype(BF16)
    return high, (v - high.astype(F32)).astype(BF16)


def as_bf16(mask):
    return jnp.where(mask, 1.0, 0.0).astype(BF16)


def iota(dims, axis):
    return lax.broadcasted_iota(jnp.int32, dims, axis)


def dispatch_body(cap, tok, router, lists, slots, send, weights, ext):
    experts, count = router.shape[0], tok.shape[0]
    top = lists.shape[0]
    rows = experts * STEP
    logits = lax.dot_general(
        router[...],
        tok[...].astype(F32),
        (((1,), (1,)), ((), ())),
        precision=lax.Precision.HIGHEST,
        preferred_element_type=F32,
    )
    which = iota((experts, count), 0)
    picked = [
        jnp.sum(jnp.where(which == lists[k : k + 1, :], logits, 0.0), axis=0, keepdims=True)
        for k in range(top)
    ]
    gates = [sigmoid(p) for p in picked]
    total = functools.reduce(jnp.add, gates)
    parts = [g / total for g in gates]
    for k in range(top):
        weights[k : k + 1, :] = parts[k]
    spread = jnp.concatenate(
        [jnp.where(which == lists[k : k + 1, :], parts[k], 0.0) for k in range(top)], axis=1
    )
    high, low = split(spread)
    slot = iota((128, count), 0)
    place = jnp.concatenate([as_bf16(slot == slots[k : k + 1, :]) for k in range(top)], axis=1)
    ext[0:count, :] = tok[...]
    ext[count:, :] = jnp.zeros((ext.shape[0] - count, ext.shape[1]), BF16)
    ext[count : count + experts, 0:128] = nt(high, place).astype(BF16)
    ext[count : count + experts, 128:256] = nt(low, place).astype(BF16)
    row = iota((rows, count), 0)
    hit = functools.reduce(
        jnp.logical_or,
        [row == lists[k : k + 1, :] * STEP + slots[k : k + 1, :] for k in range(top)],
    )
    extra = row == iota((rows, count), 1) * STEP + cap
    onehot = jnp.concatenate([as_bf16(hit), as_bf16(extra)], axis=1)
    send[...] = nn(onehot, ext[...]).astype(BF16)


def expert_body(cap, recv, gate, up, down, rows, pre_gate, pre_up, out):
    count = recv.shape[0]
    row = iota((count, 128), 0)
    block = ((row.astype(F32) + 0.5) * (1.0 / STEP)).astype(jnp.int32)
    keep = as_bf16(row - block * STEP < cap)
    x = recv[...] * jnp.concatenate([keep] * (recv.shape[1] // 128), axis=1)
    rows[...] = x
    g = nt(gate[...], x)
    u = nt(up[...], x)
    pre_gate[...] = g
    pre_up[...] = u
    hidden = (g * sigmoid(g) * u).astype(BF16)
    out[...] = tn(hidden, down[...]).astype(BF16)


def teacher_body(cap, recv, rows, out, own, other, ret):
    count = recv.shape[0]
    experts = count // STEP
    x = rows[...]
    acc = None
    for piece in (own, other):
        units = piece.shape[1] // 3
        take = lambda i: piece[:, i * units : (i + 1) * units, :].reshape(-1, x.shape[1])
        a = nt(take(0), x)
        b = nt(take(1), x)
        hidden = (a * sigmoid(a) * b).astype(BF16)
        term = tn(hidden, take(2))
        acc = term if acc is None else acc + term
    pick = as_bf16(iota((experts, count), 1) == iota((experts, count), 0) * STEP + cap)
    found = nn(pick, recv[:, 0:256]).astype(BF16)
    row = iota((count, experts), 0)
    first = iota((count, experts), 1) * STEP
    spread = as_bf16(jnp.logical_and(row >= first, row < first + STEP))
    wide = nn(spread, found)
    wide = wide[:, 0:128] + wide[:, 128:256]
    line = iota((count, 128), 0)
    block = ((line.astype(F32) + 0.5) * (1.0 / STEP)).astype(jnp.int32)
    mine = jnp.logical_and(iota((count, 128), 1) == line - block * STEP, line - block * STEP < cap)
    weight = jnp.sum(jnp.where(mine, wide, 0.0), axis=1, keepdims=True)
    ret[...] = (weight * out[...].astype(F32) - acc).astype(BF16)


def error_body(scale, ret, weights, lists, slots, send):
    top, count = lists.shape
    rows = ret.shape[0]
    row = iota((rows, count), 0)
    hits = [row == lists[k : k + 1, :] * STEP + slots[k : k + 1, :] for k in range(top)]
    onehot = as_bf16(functools.reduce(jnp.logical_or, hits))
    error = tn(onehot, ret[...]) * scale
    high, low = split(error)
    spread = functools.reduce(
        jnp.add, [jnp.where(hits[k], weights[k : k + 1, :], 0.0) for k in range(top)]
    )
    w_high, w_low = split(spread)
    left = jnp.concatenate([w_high, w_high, w_low], axis=1)
    right = jnp.concatenate([high, low, high], axis=0)
    send[...] = nn(left, right).astype(BF16)


def grad_body(place, cot, rows, pre_gate, pre_up, down, mine, theirs):
    g = pre_gate[...]
    u = pre_up[...]
    s = sigmoid(g)
    act = g * s
    grad_hidden = nt(down[...], cot[...])
    d_gate = (grad_hidden * u * s * (1.0 + g * (1.0 - s))).astype(BF16)
    d_up = (grad_hidden * act).astype(BF16)
    hidden = (act * u).astype(BF16)
    terms = (nn(d_gate, rows[...]), nn(d_up, rows[...]), nn(hidden, cot[...]))
    width = g.shape[0]
    for i, term in enumerate(terms):
        value = term.astype(BF16)
        for x in range(4):
            rel = jnp.bitwise_and(x - place[0] + 4, 3)
            for c in range(2):
                block = value[:, (2 * x + c) * 128 : (2 * x + c + 1) * 128]
                there = slice(i * width, (i + 1) * width)

                @pl.when(place[1] == c)
                def _(block=block, rel=rel, there=there):
                    mine[rel, there, :] = block

                @pl.when(place[1] != c)
                def _(block=block, rel=rel, there=there):
                    theirs[rel, there, :] = block


def fold_body(mine, got, far_up, far_down, up_late, up_now, down_now, down_late, own):
    half = far_up.shape[0]
    add = lambda k, a, b: (mine[k, a:b, :].astype(F32) + got[k, a:b, :].astype(F32)).astype(BF16)
    far_up[...] = add(2, 0, half)
    far_down[...] = add(2, half, 2 * half)
    up_late[...] = add(1, 0, half)
    up_now[...] = add(1, half, 2 * half)
    down_now[...] = add(3, 0, half)
    down_late[...] = add(3, half, 2 * half)
    own[...] = add(0, 0, 2 * half)


def add_body(a, b, c, d, first, second):
    first[...] = (a[...].astype(F32) + b[...].astype(F32)).astype(BF16)
    second[...] = (c[...].astype(F32) + d[...].astype(F32)).astype(BF16)


def finish_body(own, up_late, up_now, down_now, down_late, *outs):
    half = up_late.shape[0]
    low = own[0:half, :].astype(F32) + up_late[...].astype(F32) + down_now[...].astype(F32)
    high = own[half:, :].astype(F32) + up_now[...].astype(F32) + down_late[...].astype(F32)
    width = outs[0].shape[0]
    outs[0][...] = low[0:width]
    outs[1][0 : half - width, :] = low[width:]
    outs[1][half - width :, :] = high[0 : 2 * width - half]
    outs[2][...] = high[2 * width - half :]


def on_device(tokens, router, lists, slots, t_gate, t_up, t_down, e_gate, e_up, e_down):
    count, model = tokens.shape
    top = lists.shape[1]
    experts = router.shape[1]
    width = e_gate.shape[2]
    cap = 5 * count // experts
    rows = experts * STEP
    scale = top / math.sqrt(count * 256 * top / experts)
    core = lax.axis_index("core")
    x_at = lax.axis_index("x")

    cut = 48
    pad = ((0, 2 * cut - t_gate.shape[1]), (0, 0))
    pieces = []
    for t in (t_gate.T, t_up.T, t_down):
        whole = jnp.pad(t, pad)
        pieces.append(jnp.where(core == 0, whole[:cut], whole[cut:]))
    gathered = lax.all_gather(jnp.concatenate(pieces, axis=0), QUARTER, axis=0, tiled=False)

    lists_t, slots_t = lists.T, slots.T
    send, weights = call(
        functools.partial(dispatch_body, cap),
        [shape((rows, model), BF16), shape((top, count), F32)],
        [tokens, router.T, lists_t, slots_t],
        scratch=[pltpu.VMEM((2 * count, model), BF16)],
        flops=2 * rows * 256 * model,
        name="dispatch",
    )

    def exchange(v):
        v = v.reshape(experts, STEP, model)
        return lax.all_to_all(v, EXPERT, 0, 0, tiled=True).reshape(rows, model)

    recv = exchange(send)
    gate_t, up_t, down = e_gate[0].T, e_up[0].T, e_down[0]
    x, pre_gate, pre_up, out = call(
        functools.partial(expert_body, cap),
        [shape((rows, model), BF16), shape((width, rows), F32), shape((width, rows), F32)]
        + [shape((rows, model), BF16)],
        [recv, gate_t, up_t, down],
        flops=6 * rows * width * model,
        name="expert",
    )
    swap = [(0, 1), (1, 0)]
    other = lax.ppermute(gathered, "core", swap)
    (ret,) = call(
        functools.partial(teacher_body, cap),
        [shape((rows, model), BF16)],
        [recv, x, out, gathered, other],
        flops=6 * rows * 768 * model,
        name="teacher",
    )
    (cot_send,) = call(
        functools.partial(error_body, scale),
        [shape((rows, model), BF16)],
        [exchange(ret), weights, lists_t, slots_t],
        flops=2 * rows * 512 * model,
        name="error",
    )
    place = jnp.stack([x_at, core]).astype(jnp.int32)
    tall = 3 * width
    mine, theirs = call(
        grad_body,
        [shape((4, tall, 128), BF16)] * 2,
        [place, exchange(cot_send), x, pre_gate, pre_up, down],
        specs=[SMEM] + [VMEM] * 5,
        flops=8 * rows * width * model,
        name="grads",
    )
    got = lax.ppermute(theirs, "core", swap)
    half = tall // 2
    halves = shape((half, 128), BF16)
    far_up, far_down, up_late, up_now, down_now, down_late, own = call(
        fold_body, [halves] * 6 + [shape((tall, 128), BF16)], [mine, got], name="fold"
    )
    up = [(s, (s + 1) % 4) for s in range(4)]
    dn = [(s, (s - 1) % 4) for s in range(4)]
    a = lax.ppermute(far_up, "x", up)
    b = lax.ppermute(far_down, "x", dn)
    now_up = lax.ppermute(up_now, "x", up)
    now_dn = lax.ppermute(down_now, "x", dn)
    late_up, late_dn = call(add_body, [halves] * 2, [up_late, a, down_late, b], name="pass_on")
    late_up = lax.ppermute(late_up, "x", up)
    late_dn = lax.ppermute(late_dn, "x", dn)
    g, u, d = call(
        finish_body,
        [shape((width, 128), F32)] * 3,
        [own, late_up, now_up, now_dn, late_dn],
        name="finish",
    )
    return g.T[None], u.T[None], d[None]


def solution(mesh):
    fine = Mesh(mesh.devices.reshape(4, 2, 4, 2, 4), ALL)
    return jax.shard_map(
        on_device,
        mesh=fine,
        in_specs=(
            P(ALL, None),
            P(),
            P(ALL, None),
            P(ALL, None),
            P(None, EXPERT),
            P(None, EXPERT),
            P(EXPERT, None),
            P(EXPERT, None, None),
            P(EXPERT, None, None),
            P(EXPERT, None, None),
        ),
        out_specs=(P(EXPERT, DP, None), P(EXPERT, DP, None), P(EXPERT, None, DP)),
        check_vma=False,
    )
```

```python
import functools
import math

import jax
import jax.numpy as jnp
from jax import lax
from jax.experimental import pallas as pl
from jax.experimental.pallas import tpu as pltpu
from jax.sharding import Mesh, PartitionSpec as P

BF16 = jnp.bfloat16
F32 = jnp.float32
ALL = ("x", "core", "zq", "zp", "y")
DP = ("x", "core")
EXPERT = ("zq", "zp", "y")
VMEM = pl.BlockSpec(memory_space=pltpu.VMEM)
SMEM = pl.BlockSpec(memory_space=pltpu.SMEM)
STEP = 24


def call(body, outs, args, specs=None, scratch=(), flops=0, name=None):
    moved = sum(a.size * a.dtype.itemsize for a in args)
    moved += sum(math.prod(o.shape) * o.dtype.itemsize for o in outs)
    result = pl.pallas_call(
        body,
        out_shape=tuple(outs),
        in_specs=specs or [VMEM] * len(args),
        out_specs=tuple([VMEM] * len(outs)),
        scratch_shapes=list(scratch),
        cost_estimate=pl.CostEstimate(flops=flops, bytes_accessed=moved, transcendentals=0),
        compiler_params=pltpu.CompilerParams(vmem_limit_bytes=24 * 1024 * 1024),
        name=name,
    )(*args)
    return result


def shape(dims, dtype):
    return jax.ShapeDtypeStruct(dims, dtype)


def nt(a, b):
    return lax.dot_general(a, b, (((1,), (1,)), ((), ())), preferred_element_type=F32)


def tn(a, b):
    return lax.dot_general(a, b, (((0,), (0,)), ((), ())), preferred_element_type=F32)


def nn(a, b):
    return jnp.dot(a, b, preferred_element_type=F32)


def sigmoid(v):
    return 1.0 / (1.0 + jnp.exp(-v))


def split(v):
    high = v.astype(BF16)
    return high, (v - high.astype(F32)).astype(BF16)


def as_bf16(mask):
    return jnp.where(mask, 1.0, 0.0).astype(BF16)


def iota(dims, axis):
    return lax.broadcasted_iota(jnp.int32, dims, axis)


def dispatch_body(cap, tok, router, lists, slots, send, weights, ext):
    experts, count = router.shape[0], tok.shape[0]
    top = lists.shape[0]
    rows = experts * STEP
    logits = lax.dot_general(
        router[...],
        tok[...].astype(F32),
        (((1,), (1,)), ((), ())),
        precision=lax.Precision.HIGHEST,
        preferred_element_type=F32,
    )
    which = iota((experts, count), 0)
    picked = [
        jnp.sum(jnp.where(which == lists[k : k + 1, :], logits, 0.0), axis=0, keepdims=True)
        for k in range(top)
    ]
    gates = [sigmoid(p) for p in picked]
    total = functools.reduce(jnp.add, gates)
    parts = [g / total for g in gates]
    for k in range(top):
        weights[k : k + 1, :] = parts[k]
    spread = jnp.concatenate(
        [jnp.where(which == lists[k : k + 1, :], parts[k], 0.0) for k in range(top)], axis=1
    )
    high, low = split(spread)
    slot = iota((128, count), 0)
    place = jnp.concatenate([as_bf16(slot == slots[k : k + 1, :]) for k in range(top)], axis=1)
    ext[0:count, :] = tok[...]
    ext[count:, :] = jnp.zeros((ext.shape[0] - count, ext.shape[1]), BF16)
    ext[count : count + experts, 0:128] = nt(high, place).astype(BF16)
    ext[count : count + experts, 128:256] = nt(low, place).astype(BF16)
    row = iota((rows, count), 0)
    hit = functools.reduce(
        jnp.logical_or,
        [row == lists[k : k + 1, :] * STEP + slots[k : k + 1, :] for k in range(top)],
    )
    extra = row == iota((rows, count), 1) * STEP + cap
    onehot = jnp.concatenate([as_bf16(hit), as_bf16(extra)], axis=1)
    send[...] = nn(onehot, ext[...]).astype(BF16)


def expert_body(cap, recv, gate, up, down, rows, pre_gate, pre_up, out):
    count = recv.shape[0]
    row = iota((count, 128), 0)
    block = ((row.astype(F32) + 0.5) * (1.0 / STEP)).astype(jnp.int32)
    keep = as_bf16(row - block * STEP < cap)
    x = recv[...] * jnp.concatenate([keep] * (recv.shape[1] // 128), axis=1)
    rows[...] = x
    g = nt(gate[...], x)
    u = nt(up[...], x)
    pre_gate[...] = g
    pre_up[...] = u
    hidden = (g * sigmoid(g) * u).astype(BF16)
    out[...] = tn(hidden, down[...]).astype(BF16)


def teacher_body(cap, recv, rows, out, own, other, ret):
    count = recv.shape[0]
    experts = count // STEP
    x = rows[...]
    acc = None
    for piece in (own, other):
        units = piece.shape[1] // 3
        take = lambda i: piece[:, i * units : (i + 1) * units, :].reshape(-1, x.shape[1])
        a = nt(take(0), x)
        b = nt(take(1), x)
        hidden = (a * sigmoid(a) * b).astype(BF16)
        term = tn(hidden, take(2))
        acc = term if acc is None else acc + term
    pick = as_bf16(iota((experts, count), 1) == iota((experts, count), 0) * STEP + cap)
    found = nn(pick, recv[:, 0:256]).astype(BF16)
    row = iota((count, experts), 0)
    first = iota((count, experts), 1) * STEP
    spread = as_bf16(jnp.logical_and(row >= first, row < first + STEP))
    wide = nn(spread, found)
    wide = wide[:, 0:128] + wide[:, 128:256]
    line = iota((count, 128), 0)
    block = ((line.astype(F32) + 0.5) * (1.0 / STEP)).astype(jnp.int32)
    mine = jnp.logical_and(iota((count, 128), 1) == line - block * STEP, line - block * STEP < cap)
    weight = jnp.sum(jnp.where(mine, wide, 0.0), axis=1, keepdims=True)
    ret[...] = (weight * out[...].astype(F32) - acc).astype(BF16)


def error_body(scale, ret, weights, lists, slots, send):
    top, count = lists.shape
    rows = ret.shape[0]
    row = iota((rows, count), 0)
    hits = [row == lists[k : k + 1, :] * STEP + slots[k : k + 1, :] for k in range(top)]
    onehot = as_bf16(functools.reduce(jnp.logical_or, hits))
    error = tn(onehot, ret[...]) * scale
    high, low = split(error)
    spread = functools.reduce(
        jnp.add, [jnp.where(hits[k], weights[k : k + 1, :], 0.0) for k in range(top)]
    )
    w_high, w_low = split(spread)
    left = jnp.concatenate([w_high, w_high, w_low], axis=1)
    right = jnp.concatenate([high, low, high], axis=0)
    send[...] = nn(left, right).astype(BF16)


def grad_body(place, cot, rows, pre_gate, pre_up, down, mine, theirs):
    g = pre_gate[...]
    u = pre_up[...]
    s = sigmoid(g)
    act = g * s
    grad_hidden = nt(down[...], cot[...])
    d_gate = (grad_hidden * u * s * (1.0 + g * (1.0 - s))).astype(BF16)
    d_up = (grad_hidden * act).astype(BF16)
    hidden = (act * u).astype(BF16)
    terms = (nn(d_gate, rows[...]), nn(d_up, rows[...]), nn(hidden, cot[...]))
    width = g.shape[0]
    for i, term in enumerate(terms):
        value = term.astype(BF16)
        for x in range(4):
            rel = jnp.bitwise_and(x - place[0] + 4, 3)
            for c in range(2):
                block = value[:, (2 * x + c) * 128 : (2 * x + c + 1) * 128]
                there = slice(i * width, (i + 1) * width)

                @pl.when(place[1] == c)
                def _(block=block, rel=rel, there=there):
                    mine[rel, there, :] = block

                @pl.when(place[1] != c)
                def _(block=block, rel=rel, there=there):
                    theirs[rel, there, :] = block


def fold_body(mine, got, far_up, far_down, up_late, up_now, down_now, down_late, own):
    half = far_up.shape[0]
    add = lambda k, a, b: (mine[k, a:b, :].astype(F32) + got[k, a:b, :].astype(F32)).astype(BF16)
    far_up[...] = add(2, 0, half)
    far_down[...] = add(2, half, 2 * half)
    up_late[...] = add(1, 0, half)
    up_now[...] = add(1, half, 2 * half)
    down_now[...] = add(3, 0, half)
    down_late[...] = add(3, half, 2 * half)
    own[...] = add(0, 0, 2 * half)


def add_body(a, b, c, d, first, second):
    first[...] = (a[...].astype(F32) + b[...].astype(F32)).astype(BF16)
    second[...] = (c[...].astype(F32) + d[...].astype(F32)).astype(BF16)


def finish_body(own, up_late, up_now, down_now, down_late, *outs):
    half = up_late.shape[0]
    low = own[0:half, :].astype(F32) + up_late[...].astype(F32) + down_now[...].astype(F32)
    high = own[half:, :].astype(F32) + up_now[...].astype(F32) + down_late[...].astype(F32)
    width = outs[0].shape[0]
    outs[0][...] = low[0:width]
    outs[1][0 : half - width, :] = low[width:]
    outs[1][half - width :, :] = high[0 : 2 * width - half]
    outs[2][...] = high[2 * width - half :]


def on_device(tokens, router, lists, slots, t_gate, t_up, t_down, e_gate, e_up, e_down):
    count, model = tokens.shape
    top = lists.shape[1]
    experts = router.shape[1]
    width = e_gate.shape[2]
    cap = 5 * count // experts
    rows = experts * STEP
    scale = top / math.sqrt(count * 256 * top / experts)
    core = lax.axis_index("core")
    x_at = lax.axis_index("x")

    cut = 48
    pad = ((0, 2 * cut - t_gate.shape[1]), (0, 0))
    pieces = []
    for t in (t_gate.T, t_up.T, t_down):
        whole = jnp.pad(t, pad)
        pieces.append(jnp.where(core == 0, whole[:cut], whole[cut:]))
    shard = jnp.concatenate(pieces, axis=0)

    def shift(v, axis, size, by):
        return lax.ppermute(v, axis, [(s, (s + by) % size) for s in range(size)])

    pair = shift(shard, "zp", 2, 1)
    after = shift(shard, "y", 4, 1)
    before = shift(shard, "y", 4, -1)
    pair_after = shift(pair, "y", 4, 1)
    pair_before = shift(pair, "y", 4, -1)
    far = shift(after, "y", 4, 1)
    pair_far = shift(pair_before, "y", 4, -1)
    gathered = jnp.stack(
        [shard, pair, after, before, pair_after, pair_before, far, pair_far], axis=0
    )

    lists_t, slots_t = lists.T, slots.T
    send, weights = call(
        functools.partial(dispatch_body, cap),
        [shape((rows, model), BF16), shape((top, count), F32)],
        [tokens, router.T, lists_t, slots_t],
        scratch=[pltpu.VMEM((2 * count, model), BF16)],
        flops=2 * rows * 256 * model,
        name="dispatch",
    )

    def exchange(v):
        v = v.reshape(experts, STEP, model)
        return lax.all_to_all(v, EXPERT, 0, 0, tiled=True).reshape(rows, model)

    recv = exchange(send)
    gate_t, up_t, down = e_gate[0].T, e_up[0].T, e_down[0]
    x, pre_gate, pre_up, out = call(
        functools.partial(expert_body, cap),
        [shape((rows, model), BF16), shape((width, rows), F32), shape((width, rows), F32)]
        + [shape((rows, model), BF16)],
        [recv, gate_t, up_t, down],
        flops=6 * rows * width * model,
        name="expert",
    )
    swap = [(0, 1), (1, 0)]
    other = lax.ppermute(gathered, "core", swap)
    (ret,) = call(
        functools.partial(teacher_body, cap),
        [shape((rows, model), BF16)],
        [recv, x, out, gathered, other],
        flops=6 * rows * 768 * model,
        name="teacher",
    )
    (cot_send,) = call(
        functools.partial(error_body, scale),
        [shape((rows, model), BF16)],
        [exchange(ret), weights, lists_t, slots_t],
        flops=2 * rows * 512 * model,
        name="error",
    )
    place = jnp.stack([x_at, core]).astype(jnp.int32)
    tall = 3 * width
    mine, theirs = call(
        grad_body,
        [shape((4, tall, 128), BF16)] * 2,
        [place, exchange(cot_send), x, pre_gate, pre_up, down],
        specs=[SMEM] + [VMEM] * 5,
        flops=8 * rows * width * model,
        name="grads",
    )
    got = lax.ppermute(theirs, "core", swap)
    half = tall // 2
    halves = shape((half, 128), BF16)
    far_up, far_down, up_late, up_now, down_now, down_late, own = call(
        fold_body, [halves] * 6 + [shape((tall, 128), BF16)], [mine, got], name="fold"
    )
    up = [(s, (s + 1) % 4) for s in range(4)]
    dn = [(s, (s - 1) % 4) for s in range(4)]
    a = lax.ppermute(far_up, "x", up)
    b = lax.ppermute(far_down, "x", dn)
    now_up = lax.ppermute(up_now, "x", up)
    now_dn = lax.ppermute(down_now, "x", dn)
    late_up, late_dn = call(add_body, [halves] * 2, [up_late, a, down_late, b], name="pass_on")
    late_up = lax.ppermute(late_up, "x", up)
    late_dn = lax.ppermute(late_dn, "x", dn)
    g, u, d = call(
        finish_body,
        [shape((width, 128), F32)] * 3,
        [own, late_up, now_up, now_dn, late_dn],
        name="finish",
    )
    return g.T[None], u.T[None], d[None]


def solution(mesh):
    fine = Mesh(mesh.devices.reshape(4, 2, 4, 2, 4), ALL)
    return jax.shard_map(
        on_device,
        mesh=fine,
        in_specs=(
            P(ALL, None),
            P(),
            P(ALL, None),
            P(ALL, None),
            P(None, EXPERT),
            P(None, EXPERT),
            P(EXPERT, None),
            P(EXPERT, None, None),
            P(EXPERT, None, None),
            P(EXPERT, None, None),
        ),
        out_specs=(P(EXPERT, DP, None), P(EXPERT, DP, None), P(EXPERT, None, DP)),
        check_vma=False,
    )
```

```python
import functools
import math

import jax
import jax.numpy as jnp
from jax import lax
from jax.experimental import pallas as pl
from jax.experimental.pallas import tpu as pltpu
from jax.sharding import Mesh, PartitionSpec as P

BF16 = jnp.bfloat16
F32 = jnp.float32
ALL = ("x", "core", "zq", "zp", "y")
DP = ("x", "core")
EXPERT = ("zq", "zp", "y")
VMEM = pl.BlockSpec(memory_space=pltpu.VMEM)
HBM = pl.BlockSpec(memory_space=pltpu.MemorySpace.HBM)
GRANT_D, GRANT_F, GRANT_G = 62, 49, 24
STEP = 24


def call(body, outs, args, specs=None, out_specs=None, scratch=(), flops=0, name=None, grant=24):
    moved = sum(a.size * a.dtype.itemsize for a in args)
    moved += sum(math.prod(o.shape) * o.dtype.itemsize for o in outs)
    result = pl.pallas_call(
        body,
        out_shape=tuple(outs),
        in_specs=specs or [VMEM] * len(args),
        out_specs=tuple(out_specs or [VMEM] * len(outs)),
        scratch_shapes=list(scratch),
        cost_estimate=pl.CostEstimate(flops=flops, bytes_accessed=moved, transcendentals=0),
        compiler_params=pltpu.CompilerParams(vmem_limit_bytes=grant * 1024 * 1024),
        name=name,
    )(*args)
    return result


def shape(dims, dtype):
    return jax.ShapeDtypeStruct(dims, dtype)


def nt(a, b):
    return lax.dot_general(a, b, (((1,), (1,)), ((), ())), preferred_element_type=F32)


def tn(a, b):
    return lax.dot_general(a, b, (((0,), (0,)), ((), ())), preferred_element_type=F32)


def nn(a, b):
    return jnp.dot(a, b, preferred_element_type=F32)


def sigmoid(v):
    return 1.0 / (1.0 + jnp.exp(-v))


def split(v):
    high = v.astype(BF16)
    return high, (v - high.astype(F32)).astype(BF16)


def as_bf16(mask):
    return jnp.where(mask, 1.0, 0.0).astype(BF16)


def iota(dims, axis):
    return lax.broadcasted_iota(jnp.int32, dims, axis)


def fetch(pairs, sems):
    copies = [pltpu.make_async_copy(src, dst, sems.at[i]) for i, (src, dst) in enumerate(pairs)]
    for copy in copies:
        copy.start()
    return copies


def quotient(v, by):
    return ((v.astype(F32) + 0.5) * (1.0 / by)).astype(jnp.int32)


def dispatch_body(
    cap, tok_h, router_h, lists_h, slots_h, gate_h, up_h, down_h, send, weights, shard,
    tok, router, lists, slots, gate, up, down, ext, sems,
):
    copies = fetch(
        [(router_h, router), (tok_h, tok), (lists_h, lists), (slots_h, slots)]
        + [(gate_h, gate), (up_h, up), (down_h, down)],
        sems,
    )
    for copy in copies[:4]:
        copy.wait()
    experts, count = router.shape[0], tok.shape[0]
    top = lists.shape[0]
    rows = experts * STEP
    logits = lax.dot_general(
        router[...],
        tok[...].astype(F32),
        (((1,), (1,)), ((), ())),
        precision=lax.Precision.HIGHEST,
        preferred_element_type=F32,
    )
    which = iota((experts, count), 0)
    picked = [
        jnp.sum(jnp.where(which == lists[k : k + 1, :], logits, 0.0), axis=0, keepdims=True)
        for k in range(top)
    ]
    gates = [sigmoid(p) for p in picked]
    total = functools.reduce(jnp.add, gates)
    parts = [g / total for g in gates]
    for k in range(top):
        weights[k : k + 1, :] = parts[k]
    spread = jnp.concatenate(
        [jnp.where(which == lists[k : k + 1, :], parts[k], 0.0) for k in range(top)], axis=1
    )
    high, low = split(spread)
    slot = iota((128, count), 0)
    place = jnp.concatenate([as_bf16(slot == slots[k : k + 1, :]) for k in range(top)], axis=1)
    ext[0:count, :] = tok[...]
    ext[count:, :] = jnp.zeros((ext.shape[0] - count, ext.shape[1]), BF16)
    ext[count : count + experts, 0:128] = nt(high, place).astype(BF16)
    ext[count : count + experts, 128:256] = nt(low, place).astype(BF16)
    row = iota((rows, count), 0)
    hit = functools.reduce(
        jnp.logical_or,
        [row == lists[k : k + 1, :] * STEP + slots[k : k + 1, :] for k in range(top)],
    )
    extra = row == iota((rows, count), 1) * STEP + cap
    onehot = jnp.concatenate([as_bf16(hit), as_bf16(extra)], axis=1)
    send[...] = nn(onehot, ext[...]).astype(BF16)
    for copy in copies[4:]:
        copy.wait()
    core = lax.axis_index("core")
    cut = shard.shape[0] // 3
    for i, piece in enumerate((gate, up, down)):
        units = piece.shape[0]
        at = i * cut
        full = (units - cut) // 16 * 16

        @pl.when(core == 0)
        def _(piece=piece, at=at):
            shard[at : at + cut, :] = piece[0:cut, :]

        @pl.when(core != 0)
        def _(piece=piece, at=at, full=full, units=units):
            shard[at : at + full, :] = piece[cut : cut + full, :]
            shard[at + full : at + cut, :] = jnp.zeros((cut - full, shard.shape[1]), BF16)
            shard[at + full : at + units - cut, :] = piece[cut + full : units, :]


def packing(cap, flip):
    dims = (8 * STEP, 8 * cap) if flip else (8 * cap, 8 * STEP)
    wire, wide = iota(dims, 1 if flip else 0), iota(dims, 0 if flip else 1)
    part = quotient(wire, cap)
    block = quotient(wire, 2 * cap)
    half = part - 2 * block
    return as_bf16(wide == half * (4 * STEP) + block * STEP + wire - part * cap)


def forward_body(
    cap, recv, gate, up, down_h, own_h, other_h, rows, pre_gate, pre_up, ret,
    down, own, other, x_out, g_out, u_out, sems,
):
    copies = fetch([(down_h, down), (own_h, own), (other_h, other)], sems)
    count, model = recv.shape

    def save(src, dst, at):
        copy = pltpu.make_async_copy(src, dst, sems.at[at])
        copy.start()
        return copy

    experts = count // STEP
    line = iota((count, 128), 0)
    slot = line - quotient(line, STEP) * STEP
    keep = as_bf16(slot < cap)
    x = recv[...] * jnp.concatenate([keep] * (model // 128), axis=1)
    x_out[...] = x
    saves = [save(x_out, rows, 3)]
    pick = as_bf16(iota((experts, count), 1) == iota((experts, count), 0) * STEP + cap)
    found = nn(pick, recv[:, 0:256]).astype(BF16)
    row = iota((count, experts), 0)
    first = iota((count, experts), 1) * STEP
    spread = as_bf16(jnp.logical_and(row >= first, row < first + STEP))
    wide = nn(spread, found)
    wide = wide[:, 0:128] + wide[:, 128:256]
    mine = jnp.logical_and(iota((count, 128), 1) == slot, slot < cap)
    weight = jnp.sum(jnp.where(mine, wide, 0.0), axis=1, keepdims=True)
    g = nt(gate[...], x)
    g_out[...] = g
    saves.append(save(g_out, pre_gate, 4))
    u = nt(up[...], x)
    u_out[...] = u
    saves.append(save(u_out, pre_up, 5))
    hidden = (g * sigmoid(g) * u).astype(BF16)
    copies[0].wait()
    acc = weight * tn(hidden, down[...])
    for copy, piece in zip(copies[1:], (own, other)):
        units = piece.shape[1] // 3
        take = lambda i: piece[:, i * units : (i + 1) * units, :].reshape(-1, model)
        copy.wait()
        a = nt(take(0), x)
        b = nt(take(1), x)
        hidden = (a * sigmoid(a) * b).astype(BF16)
        acc = acc - tn(hidden, take(2))
    result = acc.astype(BF16)
    pack = packing(cap, False)
    tall = 4 * STEP
    for i in range(experts // 4):
        part = result[i * tall : (i + 1) * tall, :]
        both = jnp.concatenate([part[:, : model // 2], part[:, model // 2 :]], axis=0)
        ret[i * 8 * cap : (i + 1) * 8 * cap, :] = nn(pack, both).astype(BF16)
    for copy in saves:
        copy.wait()


def error_body(cap, scale, ret, weights, lists_h, slots_h, send, lists, slots, sems):
    copies = fetch([(lists_h, lists), (slots_h, slots)], sems)
    top, count = lists.shape
    rows, half_width = ret.shape
    row = iota((rows, count), 0)
    part = quotient(row, cap)
    half = jnp.bitwise_and(part, 1)
    key = row - cap * half
    left = half == 0
    for copy in copies:
        copy.wait()
    hits = [key == lists[k : k + 1, :] * (2 * cap) + slots[k : k + 1, :] for k in range(top)]
    hit = functools.reduce(jnp.logical_or, hits)
    value = ret[...]
    error = scale * jnp.concatenate(
        [
            tn(as_bf16(jnp.logical_and(hit, left)), value),
            tn(as_bf16(jnp.logical_and(hit, jnp.logical_not(left))), value),
        ],
        axis=1,
    )
    high, low = split(error)
    spread = functools.reduce(
        jnp.add, [jnp.where(hits[k], weights[k : k + 1, :], 0.0) for k in range(top)]
    )
    w_high, w_low = split(spread)
    lhs = jnp.concatenate([w_high, w_high, w_low], axis=1)
    rhs = jnp.concatenate([high, low, high], axis=0)
    side = jnp.concatenate([left] * (half_width // count), axis=1)
    send[...] = jnp.where(
        side, nn(lhs, rhs[:, :half_width]), nn(lhs, rhs[:, half_width:])
    ).astype(BF16)


def grad_body(cap, wire, rows, pre_gate, pre_up, down, mine, theirs, cot):
    count, model = cot.shape
    unpack = packing(cap, True)
    tall = 4 * STEP
    for i in range(count // tall):
        both = nn(unpack, wire[i * 8 * cap : (i + 1) * 8 * cap, :]).astype(BF16)
        cot[i * tall : (i + 1) * tall, : model // 2] = both[:tall]
        cot[i * tall : (i + 1) * tall, model // 2 :] = both[tall:]
    grad_hidden = nt(down[...], cot[...])
    g = pre_gate[...]
    u = pre_up[...]
    s = sigmoid(g)
    act = g * s
    d_gate = (grad_hidden * u * s * (1.0 + g * (1.0 - s))).astype(BF16)
    d_up = (grad_hidden * act).astype(BF16)
    hidden = (act * u).astype(BF16)
    terms = (nn(d_gate, rows[...]), nn(d_up, rows[...]), nn(hidden, cot[...]))
    width = g.shape[0]
    x_at, core = lax.axis_index("x"), lax.axis_index("core")
    for i, term in enumerate(terms):
        value = term.astype(BF16)
        for x in range(4):
            rel = jnp.bitwise_and(x - x_at + 4, 3)
            for c in range(2):
                block = value[:, (2 * x + c) * 128 : (2 * x + c + 1) * 128]
                there = slice(i * width, (i + 1) * width)

                @pl.when(core == c)
                def _(block=block, rel=rel, there=there):
                    mine[rel, there, :] = block

                @pl.when(core != c)
                def _(block=block, rel=rel, there=there):
                    theirs[rel, there, :] = block


def fold_body(mine, got, far_up, far_down, up_late, up_now, down_now, down_late, own):
    half = far_up.shape[0]
    add = lambda k, a, b: (mine[k, a:b, :].astype(F32) + got[k, a:b, :].astype(F32)).astype(BF16)
    far_up[...] = add(2, 0, half)
    far_down[...] = add(2, half, 2 * half)
    up_late[...] = add(1, 0, half)
    up_now[...] = add(1, half, 2 * half)
    down_now[...] = add(3, 0, half)
    down_late[...] = add(3, half, 2 * half)
    own[...] = add(0, 0, 2 * half)


def add_body(a, b, c, d, first, second):
    first[...] = (a[...].astype(F32) + b[...].astype(F32)).astype(BF16)
    second[...] = (c[...].astype(F32) + d[...].astype(F32)).astype(BF16)


def finish_body(own, up_late, up_now, down_now, down_late, *outs):
    half = up_late.shape[0]
    low = own[0:half, :].astype(F32) + up_late[...].astype(F32) + down_now[...].astype(F32)
    high = own[half:, :].astype(F32) + up_now[...].astype(F32) + down_late[...].astype(F32)
    width = outs[0].shape[0]
    outs[0][...] = low[0:width]
    outs[1][0 : half - width, :] = low[width:]
    outs[1][half - width :, :] = high[0 : 2 * width - half]
    outs[2][...] = high[2 * width - half :]


def on_device(tokens, router, lists, slots, t_gate, t_up, t_down, e_gate, e_up, e_down):
    count, model = tokens.shape
    top = lists.shape[1]
    experts = router.shape[1]
    width = e_gate.shape[2]
    cap = 5 * count // experts
    rows = experts * STEP
    scale = top / math.sqrt(count * 256 * top / experts)
    cut = 48
    lists_t, slots_t = lists.T, slots.T
    shards = [t_gate.T, t_up.T, t_down]
    send, weights, shard = call(
        functools.partial(dispatch_body, cap),
        [shape((rows, model), BF16), shape((top, count), F32), shape((3 * cut, model), BF16)],
        [tokens, router.T, lists_t, slots_t] + shards,
        specs=[HBM] * 7,
        scratch=[
            pltpu.VMEM((count, model), BF16),
            pltpu.VMEM((experts, model), F32),
            pltpu.VMEM((top, count), jnp.int32),
            pltpu.VMEM((top, count), jnp.int32),
        ]
        + [pltpu.VMEM(t.shape, BF16) for t in shards]
        + [pltpu.VMEM((2 * count, model), BF16), pltpu.SemaphoreType.DMA((7,))],
        flops=2 * rows * 256 * model,
        name="dispatch",
        grant=GRANT_D,
    )

    def shift(v, axis, size, by):
        return lax.ppermute(v, axis, [(s, (s + by) % size) for s in range(size)])

    pair = shift(shard, "zp", 2, 1)
    after = shift(shard, "y", 4, 1)
    before = shift(shard, "y", 4, -1)
    pair_after = shift(pair, "y", 4, 1)
    pair_before = shift(pair, "y", 4, -1)
    far = shift(after, "y", 4, 1)
    pair_far = shift(pair_before, "y", 4, -1)
    gathered = jnp.stack(
        [shard, pair, after, before, pair_after, pair_before, far, pair_far], axis=0
    )

    def exchange(v):
        v = v.reshape(experts, -1, v.shape[1])
        out = lax.all_to_all(v, EXPERT, 0, 0, tiled=True)
        return out.reshape(-1, v.shape[2])

    recv = exchange(send)
    gate_t, up_t, down = e_gate[0].T, e_up[0].T, e_down[0]
    weight_buf = pltpu.VMEM((width, model), BF16)
    swap = [(0, 1), (1, 0)]
    other = lax.ppermute(gathered, "core", swap)
    piece_buf = pltpu.VMEM(gathered.shape, BF16)
    x, pre_gate, pre_up, ret = call(
        functools.partial(forward_body, cap),
        [shape((rows, model), BF16), shape((width, rows), F32), shape((width, rows), F32)]
        + [shape((2 * experts * cap, model // 2), BF16)],
        [recv, gate_t, up_t, down, gathered, other],
        specs=[VMEM] * 3 + [HBM] * 3,
        out_specs=[HBM, HBM, HBM, VMEM],
        scratch=[weight_buf]
        + [piece_buf] * 2
        + [pltpu.VMEM((rows, model), BF16)]
        + [pltpu.VMEM((width, rows), F32)] * 2
        + [pltpu.SemaphoreType.DMA((6,))],
        flops=6 * rows * (width + 768) * model,
        name="forward",
        grant=GRANT_F,
    )
    index_buf = pltpu.VMEM((top, count), jnp.int32)
    (cot_send,) = call(
        functools.partial(error_body, cap, scale),
        [shape((2 * experts * cap, model // 2), BF16)],
        [exchange(ret), weights, lists_t, slots_t],
        specs=[VMEM, VMEM, HBM, HBM],
        scratch=[index_buf] * 2 + [pltpu.SemaphoreType.DMA((2,))],
        flops=2 * rows * 512 * model,
        name="error",
    )
    tall = 3 * width
    mine, theirs = call(
        functools.partial(grad_body, cap),
        [shape((4, tall, 128), BF16)] * 2,
        [exchange(cot_send), x, pre_gate, pre_up, down],
        scratch=[pltpu.VMEM((rows, model), BF16)],
        flops=8 * rows * width * model,
        name="grads",
        grant=GRANT_G,
    )
    got = lax.ppermute(theirs, "core", swap)
    half = tall // 2
    halves = shape((half, 128), BF16)
    far_up, far_down, up_late, up_now, down_now, down_late, own = call(
        fold_body, [halves] * 6 + [shape((tall, 128), BF16)], [mine, got], name="fold"
    )
    up = [(s, (s + 1) % 4) for s in range(4)]
    dn = [(s, (s - 1) % 4) for s in range(4)]
    a = lax.ppermute(far_up, "x", up)
    b = lax.ppermute(far_down, "x", dn)
    now_up = lax.ppermute(up_now, "x", up)
    now_dn = lax.ppermute(down_now, "x", dn)
    late_up, late_dn = call(add_body, [halves] * 2, [up_late, a, down_late, b], name="pass_on")
    late_up = lax.ppermute(late_up, "x", up)
    late_dn = lax.ppermute(late_dn, "x", dn)
    g, u, d = call(
        finish_body,
        [shape((width, 128), F32)] * 3,
        [own, late_up, now_up, now_dn, late_dn],
        name="finish",
    )
    return g.T[None], u.T[None], d[None]


def solution(mesh):
    fine = Mesh(mesh.devices.reshape(4, 2, 4, 2, 4), ALL)
    return jax.shard_map(
        on_device,
        mesh=fine,
        in_specs=(
            P(ALL, None),
            P(),
            P(ALL, None),
            P(ALL, None),
            P(None, EXPERT),
            P(None, EXPERT),
            P(EXPERT, None),
            P(EXPERT, None, None),
            P(EXPERT, None, None),
            P(EXPERT, None, None),
        ),
        out_specs=(P(EXPERT, DP, None), P(EXPERT, DP, None), P(EXPERT, None, DP)),
        check_vma=False,
    )
```

```python
import functools
import math

import jax
import jax.numpy as jnp
from jax import lax
from jax.experimental import pallas as pl
from jax.experimental.pallas import tpu as pltpu
from jax.sharding import Mesh, PartitionSpec as P


BF16 = jnp.bfloat16
F32 = jnp.float32
ALL = ("x", "core", "zq", "zp", "y")
DP = ("x", "core")
EXPERT = ("zq", "zp", "y")
VMEM = pl.BlockSpec(memory_space=pltpu.VMEM)
HBM = pl.BlockSpec(memory_space=pltpu.MemorySpace.HBM)
GRANT_D, GRANT_F, GRANT_G = 62, 49, 24
STEP = 24


def call(body, outs, args, specs=None, out_specs=None, scratch=(), flops=0, grant=24):
    moved = sum(a.size * a.dtype.itemsize for a in args)
    moved += sum(math.prod(o.shape) * o.dtype.itemsize for o in outs)
    return pl.pallas_call(
        body,
        out_shape=tuple(outs),
        in_specs=specs or [VMEM] * len(args),
        out_specs=tuple(out_specs or [VMEM] * len(outs)),
        scratch_shapes=list(scratch),
        cost_estimate=pl.CostEstimate(flops=flops, bytes_accessed=moved, transcendentals=0),
        compiler_params=pltpu.CompilerParams(vmem_limit_bytes=grant * 1024 * 1024),
    )(*args)


def shape(dims, dtype):
    return jax.ShapeDtypeStruct(dims, dtype)


def nt(a, b):
    return lax.dot_general(a, b, (((1,), (1,)), ((), ())), preferred_element_type=F32)


def tn(a, b):
    return lax.dot_general(a, b, (((0,), (0,)), ((), ())), preferred_element_type=F32)


def nn(a, b):
    return jnp.dot(a, b, preferred_element_type=F32)


def sigmoid(v):
    return 1.0 / (1.0 + jnp.exp(-v))


def split(v):
    high = v.astype(BF16)
    return high, (v - high.astype(F32)).astype(BF16)


def as_bf16(mask):
    return jnp.where(mask, 1.0, 0.0).astype(BF16)


def iota(dims, axis):
    return lax.broadcasted_iota(jnp.int32, dims, axis)


def fetch(pairs, sems):
    copies = [pltpu.make_async_copy(src, dst, sems.at[i]) for i, (src, dst) in enumerate(pairs)]
    for copy in copies:
        copy.start()
    return copies


def quotient(v, by):
    return ((v.astype(F32) + 0.5) * (1.0 / by)).astype(jnp.int32)


def dispatch_body(
    cap, tok_h, router_h, lists_h, slots_h, gate_h, up_h, down_h, send, weights, shard,
    tok, router, lists, slots, gate, up, down, ext, sems,
):
    copies = fetch(
        [(router_h, router), (tok_h, tok), (lists_h, lists), (slots_h, slots)]
        + [(gate_h, gate), (up_h, up), (down_h, down)],
        sems,
    )
    for copy in copies[:4]:
        copy.wait()
    experts, count = router.shape[0], tok.shape[0]
    top = lists.shape[0]
    rows = experts * STEP
    logits = lax.dot_general(
        router[...],
        tok[...].astype(F32),
        (((1,), (1,)), ((), ())),
        precision=lax.Precision.HIGHEST,
        preferred_element_type=F32,
    )
    which = iota((experts, count), 0)
    picked = [
        jnp.sum(jnp.where(which == lists[k : k + 1, :], logits, 0.0), axis=0, keepdims=True)
        for k in range(top)
    ]
    gates = [sigmoid(p) for p in picked]
    total = functools.reduce(jnp.add, gates)
    parts = [g / total for g in gates]
    for k in range(top):
        weights[k : k + 1, :] = parts[k]
    spread = jnp.concatenate(
        [jnp.where(which == lists[k : k + 1, :], parts[k], 0.0) for k in range(top)], axis=1
    )
    high, low = split(spread)
    slot = iota((128, count), 0)
    place = jnp.concatenate([as_bf16(slot == slots[k : k + 1, :]) for k in range(top)], axis=1)
    ext[0:count, :] = tok[...]
    ext[count:, :] = jnp.zeros((ext.shape[0] - count, ext.shape[1]), BF16)
    ext[count : count + experts, 0:128] = nt(high, place).astype(BF16)
    ext[count : count + experts, 128:256] = nt(low, place).astype(BF16)
    row = iota((rows, count), 0)
    hit = functools.reduce(
        jnp.logical_or,
        [row == lists[k : k + 1, :] * STEP + slots[k : k + 1, :] for k in range(top)],
    )
    extra = row == iota((rows, count), 1) * STEP + cap
    onehot = jnp.concatenate([as_bf16(hit), as_bf16(extra)], axis=1)
    send[...] = nn(onehot, ext[...]).astype(BF16)
    for copy in copies[4:]:
        copy.wait()
    core = lax.axis_index("core")
    cut = shard.shape[0] // 3
    for i, piece in enumerate((gate, up, down)):
        units = piece.shape[0]
        at = i * cut
        full = (units - cut) // 16 * 16

        @pl.when(core == 0)
        def _(piece=piece, at=at):
            shard[at : at + cut, :] = piece[0:cut, :]

        @pl.when(core != 0)
        def _(piece=piece, at=at, full=full, units=units):
            shard[at : at + full, :] = piece[cut : cut + full, :]
            shard[at + full : at + cut, :] = jnp.zeros((cut - full, shard.shape[1]), BF16)
            shard[at + full : at + units - cut, :] = piece[cut + full : units, :]


def packing(cap, flip):
    dims = (8 * STEP, 8 * cap) if flip else (8 * cap, 8 * STEP)
    wire, wide = iota(dims, 1 if flip else 0), iota(dims, 0 if flip else 1)
    part = quotient(wire, cap)
    block = quotient(wire, 2 * cap)
    half = part - 2 * block
    return as_bf16(wide == half * (4 * STEP) + block * STEP + wire - part * cap)


def forward_body(
    cap, recv, gate, up, down_h, own_h, other_h, rows, pre_gate, pre_up, ret,
    down, own, other, x_out, g_out, u_out, sems,
):
    copies = fetch([(down_h, down), (own_h, own), (other_h, other)], sems)
    count, model = recv.shape

    def save(src, dst, at):
        copy = pltpu.make_async_copy(src, dst, sems.at[at])
        copy.start()
        return copy

    experts = count // STEP
    line = iota((count, 128), 0)
    slot = line - quotient(line, STEP) * STEP
    keep = as_bf16(slot < cap)
    x = recv[...] * jnp.concatenate([keep] * (model // 128), axis=1)
    x_out[...] = x
    saves = [save(x_out, rows, 3)]
    pick = as_bf16(iota((experts, count), 1) == iota((experts, count), 0) * STEP + cap)
    found = nn(pick, recv[:, 0:256]).astype(BF16)
    row = iota((count, experts), 0)
    first = iota((count, experts), 1) * STEP
    spread = as_bf16(jnp.logical_and(row >= first, row < first + STEP))
    wide = nn(spread, found)
    wide = wide[:, 0:128] + wide[:, 128:256]
    mine = jnp.logical_and(iota((count, 128), 1) == slot, slot < cap)
    weight = jnp.sum(jnp.where(mine, wide, 0.0), axis=1, keepdims=True)
    g = nt(gate[...], x)
    g_out[...] = g
    saves.append(save(g_out, pre_gate, 4))
    u = nt(up[...], x)
    u_out[...] = u
    saves.append(save(u_out, pre_up, 5))
    hidden = (g * sigmoid(g) * u).astype(BF16)
    copies[0].wait()
    acc = weight * tn(hidden, down[...])
    for copy, piece in zip(copies[1:], (own, other)):
        units = piece.shape[1] // 3
        take = lambda i: piece[:, i * units : (i + 1) * units, :].reshape(-1, model)
        copy.wait()
        a = nt(take(0), x)
        b = nt(take(1), x)
        hidden = (a * sigmoid(a) * b).astype(BF16)
        acc = acc - tn(hidden, take(2))
    result = acc.astype(BF16)
    pack = packing(cap, False)
    tall = 4 * STEP
    for i in range(experts // 4):
        part = result[i * tall : (i + 1) * tall, :]
        both = jnp.concatenate([part[:, : model // 2], part[:, model // 2 :]], axis=0)
        ret[i * 8 * cap : (i + 1) * 8 * cap, :] = nn(pack, both).astype(BF16)
    for copy in saves:
        copy.wait()


def error_body(cap, scale, ret, weights, lists_h, slots_h, send, lists, slots, sems):
    copies = fetch([(lists_h, lists), (slots_h, slots)], sems)
    top, count = lists.shape
    rows, half_width = ret.shape
    row = iota((rows, count), 0)
    part = quotient(row, cap)
    half = jnp.bitwise_and(part, 1)
    key = row - cap * half
    left = half == 0
    for copy in copies:
        copy.wait()
    hits = [key == lists[k : k + 1, :] * (2 * cap) + slots[k : k + 1, :] for k in range(top)]
    hit = functools.reduce(jnp.logical_or, hits)
    value = ret[...]
    error = scale * jnp.concatenate(
        [
            tn(as_bf16(jnp.logical_and(hit, left)), value),
            tn(as_bf16(jnp.logical_and(hit, jnp.logical_not(left))), value),
        ],
        axis=1,
    )
    high, low = split(error)
    spread = functools.reduce(
        jnp.add, [jnp.where(hits[k], weights[k : k + 1, :], 0.0) for k in range(top)]
    )
    w_high, w_low = split(spread)
    lhs = jnp.concatenate([w_high, w_high, w_low], axis=1)
    rhs = jnp.concatenate([high, low, high], axis=0)
    side = jnp.concatenate([left] * (half_width // count), axis=1)
    send[...] = jnp.where(
        side, nn(lhs, rhs[:, :half_width]), nn(lhs, rhs[:, half_width:])
    ).astype(BF16)


def chunk(parts, rows, cot, rels, puts):
    core, x_at = lax.axis_index("core"), lax.axis_index("x")

    def columns(ref):
        pieces = []
        for rel in rels:
            first = pl.multiple_of(jnp.bitwise_and(x_at + rel, 3) * 256, 256)
            pieces.append(ref[:, pl.ds(first, 256)])
        return jnp.concatenate(pieces, axis=1)

    side = columns(rows)
    width = parts[0].shape[0]
    for i, part in enumerate(parts):
        value = nn(part, columns(cot) if i == 2 else side).astype(BF16)
        at = slice(i * width, (i + 1) * width)
        for j, (mine, theirs) in enumerate(puts):
            left = value[:, j * 256 : j * 256 + 128]
            right = value[:, j * 256 + 128 : (j + 1) * 256]

            @pl.when(core == 0)
            def _(left=left, right=right, at=at, mine=mine, theirs=theirs):
                mine(at, left)
                theirs(at, right)

            @pl.when(core != 0)
            def _(left=left, right=right, at=at, mine=mine, theirs=theirs):
                mine(at, right)
                theirs(at, left)


def putter(ref, at=None):
    def put(rows, value):
        if at is None:
            ref[rows, :] = value
        else:
            ref[at, rows, :] = value

    return put


def grad_body(cap, wire, rows, pre_gate, pre_up, down, d_gate, d_up, hidden, cot, mine, theirs):
    count, model = cot.shape
    unpack = packing(cap, True)
    tall = 4 * STEP
    for i in range(count // tall):
        both = nn(unpack, wire[i * 8 * cap : (i + 1) * 8 * cap, :]).astype(BF16)
        cot[i * tall : (i + 1) * tall, : model // 2] = both[:tall]
        cot[i * tall : (i + 1) * tall, model // 2 :] = both[tall:]
    grad_hidden = nt(down[...], cot[...])
    g = pre_gate[...]
    u = pre_up[...]
    s = sigmoid(g)
    act = g * s
    parts = (
        (grad_hidden * u * s * (1.0 + g * (1.0 - s))).astype(BF16),
        (grad_hidden * act).astype(BF16),
        (act * u).astype(BF16),
    )
    for ref, value in zip((d_gate, d_up, hidden), parts):
        ref[...] = value
    chunk(parts, rows, cot, (2,), [(putter(mine), putter(theirs))])


def near_body(d_gate, d_up, hidden, rows, cot, mine, theirs):
    parts = (d_gate[...], d_up[...], hidden[...])
    puts = [(putter(mine, at), putter(theirs, at)) for at in range(2)]
    chunk(parts, rows, cot, (1, 3), puts)


def own_body(d_gate, d_up, hidden, rows, cot, mine, theirs):
    parts = (d_gate[...], d_up[...], hidden[...])
    chunk(parts, rows, cot, (0,), [(putter(mine), putter(theirs))])


def plus(a, b):
    return (a.astype(F32) + b.astype(F32)).astype(BF16)


def far_body(mine, got, up, down):
    half = up.shape[0]
    up[...] = plus(mine[:half, :], got[:half, :])
    down[...] = plus(mine[half:, :], got[half:, :])


def fold_body(mine, got, up_late, up_now, down_now, down_late):
    half = up_late.shape[0]
    up_late[...] = plus(mine[0, :half, :], got[0, :half, :])
    up_now[...] = plus(mine[0, half:, :], got[0, half:, :])
    down_now[...] = plus(mine[1, :half, :], got[1, :half, :])
    down_late[...] = plus(mine[1, half:, :], got[1, half:, :])


def add_body(a, b, c, d, first, second):
    first[...] = plus(a[...], b[...])
    second[...] = plus(c[...], d[...])


def finish_body(mine, got, up_late, up_now, down_now, down_late, *outs):
    half = up_late.shape[0]
    add = lambda *values: functools.reduce(jnp.add, [v.astype(F32) for v in values])
    low = add(mine[:half, :], got[:half, :], up_late[...], down_now[...])
    high = add(mine[half:, :], got[half:, :], up_now[...], down_late[...])
    width = outs[0].shape[0]
    outs[0][...] = low[0:width]
    outs[1][0 : half - width, :] = low[width:]
    outs[1][half - width :, :] = high[0 : 2 * width - half]
    outs[2][...] = high[2 * width - half :]


def on_device(tokens, router, lists, slots, t_gate, t_up, t_down, e_gate, e_up, e_down):
    count, model = tokens.shape
    top = lists.shape[1]
    experts = router.shape[1]
    width = e_gate.shape[2]
    cap = 5 * count // experts
    rows = experts * STEP
    scale = top / math.sqrt(count * 256 * top / experts)
    cut = 48
    lists_t, slots_t = lists.T, slots.T
    shards = [t_gate.T, t_up.T, t_down]
    send, weights, shard = call(
        functools.partial(dispatch_body, cap),
        [shape((rows, model), BF16), shape((top, count), F32), shape((3 * cut, model), BF16)],
        [tokens, router.T, lists_t, slots_t] + shards,
        specs=[HBM] * 7,
        scratch=[
            pltpu.VMEM((count, model), BF16),
            pltpu.VMEM((experts, model), F32),
            pltpu.VMEM((top, count), jnp.int32),
            pltpu.VMEM((top, count), jnp.int32),
        ]
        + [pltpu.VMEM(t.shape, BF16) for t in shards]
        + [pltpu.VMEM((2 * count, model), BF16), pltpu.SemaphoreType.DMA((7,))],
        flops=2 * rows * 256 * model,
        grant=GRANT_D,
    )

    def shift(v, axis, size, by):
        return lax.ppermute(v, axis, [(s, (s + by) % size) for s in range(size)])

    pair = shift(shard, "zp", 2, 1)
    after = shift(shard, "y", 4, 1)
    before = shift(shard, "y", 4, -1)
    pair_after = shift(pair, "y", 4, 1)
    pair_before = shift(pair, "y", 4, -1)
    far = shift(after, "y", 4, 1)
    pair_far = shift(pair_before, "y", 4, -1)
    gathered = jnp.stack(
        [shard, pair, after, before, pair_after, pair_before, far, pair_far], axis=0
    )

    def exchange(v):
        v = v.reshape(experts, -1, v.shape[1])
        out = lax.all_to_all(v, EXPERT, 0, 0, tiled=True)
        return out.reshape(-1, v.shape[2])

    recv = exchange(send)
    gate_t, up_t, down = e_gate[0].T, e_up[0].T, e_down[0]
    weight_buf = pltpu.VMEM((width, model), BF16)
    swap = [(0, 1), (1, 0)]
    other = lax.ppermute(gathered, "core", swap)
    piece_buf = pltpu.VMEM(gathered.shape, BF16)
    x, pre_gate, pre_up, ret = call(
        functools.partial(forward_body, cap),
        [shape((rows, model), BF16), shape((width, rows), F32), shape((width, rows), F32)]
        + [shape((2 * experts * cap, model // 2), BF16)],
        [recv, gate_t, up_t, down, gathered, other],
        specs=[VMEM] * 3 + [HBM] * 3,
        out_specs=[HBM, HBM, HBM, VMEM],
        scratch=[weight_buf]
        + [piece_buf] * 2
        + [pltpu.VMEM((rows, model), BF16)]
        + [pltpu.VMEM((width, rows), F32)] * 2
        + [pltpu.SemaphoreType.DMA((6,))],
        flops=6 * rows * (width + 768) * model,
        grant=GRANT_F,
    )
    index_buf = pltpu.VMEM((top, count), jnp.int32)
    (cot_send,) = call(
        functools.partial(error_body, cap, scale),
        [shape((2 * experts * cap, model // 2), BF16)],
        [exchange(ret), weights, lists_t, slots_t],
        specs=[VMEM, VMEM, HBM, HBM],
        scratch=[index_buf] * 2 + [pltpu.SemaphoreType.DMA((2,))],
        flops=2 * rows * 512 * model,
    )
    tall = 3 * width
    side = shape((width, rows), BF16)
    one, two = shape((tall, 128), BF16), shape((2, tall, 128), BF16)
    d_gate, d_up, hidden, cot, far_mine, far_theirs = call(
        functools.partial(grad_body, cap),
        [side] * 3 + [shape((rows, model), BF16)] + [one] * 2,
        [exchange(cot_send), x, pre_gate, pre_up, down],
        flops=4 * rows * width * model,
        grant=GRANT_G,
    )
    far_got = lax.ppermute(far_theirs, "core", swap)
    parts = [d_gate, d_up, hidden, x, cot]
    mine, theirs = call(near_body, [two] * 2, parts, flops=3 * rows * width * model, grant=GRANT_G)
    got = lax.ppermute(theirs, "core", swap)
    half = tall // 2
    halves = shape((half, 128), BF16)
    up = [(s, (s + 1) % 4) for s in range(4)]
    dn = [(s, (s - 1) % 4) for s in range(4)]
    far_up, far_down = call(far_body, [halves] * 2, [far_mine, far_got])
    a = lax.ppermute(far_up, "x", up)
    b = lax.ppermute(far_down, "x", dn)
    up_late, up_now, down_now, down_late = call(fold_body, [halves] * 4, [mine, got])
    now_up = lax.ppermute(up_now, "x", up)
    now_dn = lax.ppermute(down_now, "x", dn)
    own_mine, own_theirs = call(
        own_body, [one] * 2, parts, flops=3 * rows * width * model // 2, grant=GRANT_G
    )
    own_got = lax.ppermute(own_theirs, "core", swap)
    late_up, late_dn = call(add_body, [halves] * 2, [up_late, a, down_late, b])
    late_up = lax.ppermute(late_up, "x", up)
    late_dn = lax.ppermute(late_dn, "x", dn)
    g, u, d = call(
        finish_body,
        [shape((width, 128), F32)] * 3,
        [own_mine, own_got, late_up, now_up, now_dn, late_dn],
    )
    return g.T[None], u.T[None], d[None]


def solution(mesh):
    fine = Mesh(mesh.devices.reshape(4, 2, 4, 2, 4), ALL)

    return jax.shard_map(
        on_device,
        mesh=fine,
        in_specs=(
            P(ALL, None),
            P(),
            P(ALL, None),
            P(ALL, None),
            P(None, EXPERT),
            P(None, EXPERT),
            P(EXPERT, None),
            P(EXPERT, None, None),
            P(EXPERT, None, None),
            P(EXPERT, None, None),
        ),
        out_specs=(P(EXPERT, DP, None), P(EXPERT, DP, None), P(EXPERT, None, DP)),
        check_vma=False,
    )
```

```python
import functools
import math

import jax
import jax.numpy as jnp
from jax import lax
from jax.experimental import pallas as pl
from jax.experimental.pallas import tpu as pltpu
from jax.sharding import Mesh, PartitionSpec as P


BF16 = jnp.bfloat16
F32 = jnp.float32
ALL = ("x", "core", "zq", "zp", "y")
DP = ("x", "core")
EXPERT = ("zq", "zp", "y")
VMEM = pl.BlockSpec(memory_space=pltpu.VMEM)
HBM = pl.BlockSpec(memory_space=pltpu.MemorySpace.HBM)
GRANT_D, GRANT_F, GRANT_G = 62, 49, 24
STEP = 24


def call(body, outs, args, specs=None, out_specs=None, scratch=(), flops=0, grant=24):
    moved = sum(a.size * a.dtype.itemsize for a in args)
    moved += sum(math.prod(o.shape) * o.dtype.itemsize for o in outs)
    return pl.pallas_call(
        body,
        out_shape=tuple(outs),
        in_specs=specs or [VMEM] * len(args),
        out_specs=tuple(out_specs or [VMEM] * len(outs)),
        scratch_shapes=list(scratch),
        cost_estimate=pl.CostEstimate(flops=flops, bytes_accessed=moved, transcendentals=0),
        compiler_params=pltpu.CompilerParams(vmem_limit_bytes=grant * 1024 * 1024),
    )(*args)


def shape(dims, dtype):
    return jax.ShapeDtypeStruct(dims, dtype)


def nt(a, b):
    return lax.dot_general(a, b, (((1,), (1,)), ((), ())), preferred_element_type=F32)


def tn(a, b):
    return lax.dot_general(a, b, (((0,), (0,)), ((), ())), preferred_element_type=F32)


def nn(a, b):
    return jnp.dot(a, b, preferred_element_type=F32)


def sigmoid(v):
    return 1.0 / (1.0 + jnp.exp(-v))


def split(v):
    high = v.astype(BF16)
    return high, (v - high.astype(F32)).astype(BF16)


def as_bf16(mask):
    return jnp.where(mask, 1.0, 0.0).astype(BF16)


def iota(dims, axis):
    return lax.broadcasted_iota(jnp.int32, dims, axis)


def fetch(pairs, sems):
    copies = [pltpu.make_async_copy(src, dst, sems.at[i]) for i, (src, dst) in enumerate(pairs)]
    for copy in copies:
        copy.start()
    return copies


def quotient(v, by):
    return ((v.astype(F32) + 0.5) * (1.0 / by)).astype(jnp.int32)


def dispatch_body(
    cap, tok_h, router_h, lists_h, slots_h, gate_h, up_h, down_h, send, weights, shard,
    tok, router, lists, slots, gate, up, down, ext, sems,
):
    copies = fetch(
        [(router_h, router), (tok_h, tok), (lists_h, lists), (slots_h, slots)]
        + [(gate_h, gate), (up_h, up), (down_h, down)],
        sems,
    )
    for copy in copies[:4]:
        copy.wait()
    experts, count = router.shape[0], tok.shape[0]
    top = lists.shape[0]
    rows = experts * STEP
    logits = lax.dot_general(
        router[...],
        tok[...].astype(F32),
        (((1,), (1,)), ((), ())),
        precision=lax.Precision.HIGHEST,
        preferred_element_type=F32,
    )
    which = iota((experts, count), 0)
    picked = [
        jnp.sum(jnp.where(which == lists[k : k + 1, :], logits, 0.0), axis=0, keepdims=True)
        for k in range(top)
    ]
    gates = [sigmoid(p) for p in picked]
    total = functools.reduce(jnp.add, gates)
    parts = [g / total for g in gates]
    for k in range(top):
        weights[k : k + 1, :] = parts[k]
    spread = jnp.concatenate(
        [jnp.where(which == lists[k : k + 1, :], parts[k], 0.0) for k in range(top)], axis=1
    )
    high, low = split(spread)
    slot = iota((128, count), 0)
    place = jnp.concatenate([as_bf16(slot == slots[k : k + 1, :]) for k in range(top)], axis=1)
    ext[0:count, :] = tok[...]
    ext[count:, :] = jnp.zeros((ext.shape[0] - count, ext.shape[1]), BF16)
    ext[count : count + experts, 0:128] = nt(high, place).astype(BF16)
    ext[count : count + experts, 128:256] = nt(low, place).astype(BF16)
    row = iota((rows, count), 0)
    hit = functools.reduce(
        jnp.logical_or,
        [row == lists[k : k + 1, :] * STEP + slots[k : k + 1, :] for k in range(top)],
    )
    extra = row == iota((rows, count), 1) * STEP + cap
    onehot = jnp.concatenate([as_bf16(hit), as_bf16(extra)], axis=1)
    send[...] = nn(onehot, ext[...]).astype(BF16)
    for copy in copies[4:]:
        copy.wait()
    core = lax.axis_index("core")
    cut = shard.shape[0] // 3
    for i, piece in enumerate((gate, up, down)):
        units = piece.shape[0]
        at = i * cut
        full = (units - cut) // 16 * 16

        @pl.when(core == 0)
        def _(piece=piece, at=at):
            shard[at : at + cut, :] = piece[0:cut, :]

        @pl.when(core != 0)
        def _(piece=piece, at=at, full=full, units=units):
            shard[at : at + full, :] = piece[cut : cut + full, :]
            shard[at + full : at + cut, :] = jnp.zeros((cut - full, shard.shape[1]), BF16)
            shard[at + full : at + units - cut, :] = piece[cut + full : units, :]


def packing(cap, flip):
    dims = (8 * STEP, 8 * cap) if flip else (8 * cap, 8 * STEP)
    wire, wide = iota(dims, 1 if flip else 0), iota(dims, 0 if flip else 1)
    part = quotient(wire, cap)
    block = quotient(wire, 2 * cap)
    half = part - 2 * block
    return as_bf16(wide == half * (4 * STEP) + block * STEP + wire - part * cap)


def forward_body(
    cap, recv, gate, up, down_h, own_h, own_far_h, other_h, other_far_h, rows, slope, act, middle,
    ret, down, piece, x_out, slope_out, act_out, middle_out, sems,
):
    pairs, first_unit = [(down_h, down)], 0
    for source in (own_h, own_far_h, other_h, other_far_h):
        pairs.append((source, piece.at[first_unit : first_unit + source.shape[0]]))
        first_unit += source.shape[0]
    copies = fetch(pairs, sems)
    count, model = recv.shape

    def save(src, dst, at):
        copy = pltpu.make_async_copy(src, dst, sems.at[at])
        copy.start()
        return copy

    experts = count // STEP
    line = iota((count, 128), 0)
    slot = line - quotient(line, STEP) * STEP
    keep = as_bf16(slot < cap)
    x = recv[...] * jnp.concatenate([keep] * (model // 128), axis=1)
    x_out[...] = x
    saves = [save(x_out, rows, 5)]
    pick = as_bf16(iota((experts, count), 1) == iota((experts, count), 0) * STEP + cap)
    found = nn(pick, recv[:, 0:256]).astype(BF16)
    row = iota((count, experts), 0)
    first = iota((count, experts), 1) * STEP
    spread = as_bf16(jnp.logical_and(row >= first, row < first + STEP))
    wide = nn(spread, found)
    wide = wide[:, 0:128] + wide[:, 128:256]
    mine = jnp.logical_and(iota((count, 128), 1) == slot, slot < cap)
    weight = jnp.sum(jnp.where(mine, wide, 0.0), axis=1, keepdims=True)
    g = nt(gate[...], x)
    u = nt(up[...], x)
    s = sigmoid(g)
    a = g * s
    act_out[...] = a
    saves.append(save(act_out, act, 6))
    slope_out[...] = u * s * (1.0 + g * (1.0 - s))
    saves.append(save(slope_out, slope, 7))
    hidden = (a * u).astype(BF16)
    middle_out[...] = hidden
    saves.append(save(middle_out, middle, 8))
    copies[0].wait()
    acc = weight * tn(hidden, down[...])
    units = piece.shape[1] // 3
    take = lambda i: piece[:, i * units : (i + 1) * units, :].reshape(-1, model)
    for copy in copies[1:]:
        copy.wait()
    a = nt(take(0), x)
    b = nt(take(1), x)
    hidden = (a * sigmoid(a) * b).astype(BF16)
    acc = acc - tn(hidden, take(2))
    result = acc.astype(BF16)
    pack = packing(cap, False)
    tall = 4 * STEP
    for i in range(experts // 4):
        part = result[i * tall : (i + 1) * tall, :]
        both = jnp.concatenate([part[:, : model // 2], part[:, model // 2 :]], axis=0)
        ret[i * 8 * cap : (i + 1) * 8 * cap, :] = nn(pack, both).astype(BF16)
    for copy in saves:
        copy.wait()


def error_body(cap, scale, ret, weights, lists_h, slots_h, send, lists, slots, sems):
    copies = fetch([(lists_h, lists), (slots_h, slots)], sems)
    top, count = lists.shape
    rows, half_width = ret.shape
    row = iota((rows, count), 0)
    part = quotient(row, cap)
    half = jnp.bitwise_and(part, 1)
    key = row - cap * half
    left = half == 0
    for copy in copies:
        copy.wait()
    hits = [key == lists[k : k + 1, :] * (2 * cap) + slots[k : k + 1, :] for k in range(top)]
    hit = functools.reduce(jnp.logical_or, hits)
    value = ret[...]
    error = scale * jnp.concatenate(
        [
            tn(as_bf16(jnp.logical_and(hit, left)), value),
            tn(as_bf16(jnp.logical_and(hit, jnp.logical_not(left))), value),
        ],
        axis=1,
    )
    high, low = split(error)
    spread = functools.reduce(
        jnp.add, [jnp.where(hits[k], weights[k : k + 1, :], 0.0) for k in range(top)]
    )
    w_high, w_low = split(spread)
    lhs = jnp.concatenate([w_high, w_high, w_low], axis=1)
    rhs = jnp.concatenate([high, low, high], axis=0)
    side = jnp.concatenate([left] * (half_width // count), axis=1)
    send[...] = jnp.where(
        side, nn(lhs, rhs[:, :half_width]), nn(lhs, rhs[:, half_width:])
    ).astype(BF16)


def chunk(parts, rows, cot, rels, puts):
    core, x_at = lax.axis_index("core"), lax.axis_index("x")

    def columns(ref):
        pieces = []
        for rel in rels:
            first = pl.multiple_of(jnp.bitwise_and(x_at + rel, 3) * 256, 256)
            pieces.append(ref[:, pl.ds(first, 256)])
        return jnp.concatenate(pieces, axis=1)

    side = columns(rows)
    width = parts[0].shape[0]
    for i, part in enumerate(parts):
        value = nn(part, columns(cot) if i == 2 else side).astype(BF16)
        at = slice(i * width, (i + 1) * width)
        for j, (mine, theirs) in enumerate(puts):
            left = value[:, j * 256 : j * 256 + 128]
            right = value[:, j * 256 + 128 : (j + 1) * 256]

            @pl.when(core == 0)
            def _(left=left, right=right, at=at, mine=mine, theirs=theirs):
                mine(at, left)
                theirs(at, right)

            @pl.when(core != 0)
            def _(left=left, right=right, at=at, mine=mine, theirs=theirs):
                mine(at, right)
                theirs(at, left)


def putter(ref, at=None):
    def put(rows, value):
        if at is None:
            ref[rows, :] = value
        else:
            ref[at, rows, :] = value

    return put


def grad_body(cap, wire, rows, slope, act, hidden, down, d_gate, d_up, cot, mine, theirs):
    count, model = cot.shape
    unpack = packing(cap, True)
    tall = 4 * STEP
    for i in range(count // tall):
        both = nn(unpack, wire[i * 8 * cap : (i + 1) * 8 * cap, :]).astype(BF16)
        cot[i * tall : (i + 1) * tall, : model // 2] = both[:tall]
        cot[i * tall : (i + 1) * tall, model // 2 :] = both[tall:]
    grad_hidden = nt(down[...], cot[...])
    d_gate[...] = (grad_hidden * slope[...]).astype(BF16)
    d_up[...] = (grad_hidden * act[...]).astype(BF16)
    parts = (d_gate[...], d_up[...], hidden[...])
    chunk(parts, rows, cot, (2,), [(putter(mine), putter(theirs))])


def near_body(d_gate, d_up, hidden, rows, cot, mine, theirs):
    parts = (d_gate[...], d_up[...], hidden[...])
    puts = [(putter(mine, at), putter(theirs, at)) for at in range(2)]
    chunk(parts, rows, cot, (1, 3), puts)


def own_body(d_gate, d_up, hidden, rows, cot, mine, theirs):
    parts = (d_gate[...], d_up[...], hidden[...])
    chunk(parts, rows, cot, (0,), [(putter(mine), putter(theirs))])


def plus(a, b):
    return (a.astype(F32) + b.astype(F32)).astype(BF16)


def far_body(mine, got, up, down):
    half = up.shape[0]
    up[...] = plus(mine[:half, :], got[:half, :])
    down[...] = plus(mine[half:, :], got[half:, :])


def fold_body(mine, got, up_late, up_now, down_now, down_late):
    half = up_late.shape[0]
    up_late[...] = plus(mine[0, :half, :], got[0, :half, :])
    up_now[...] = plus(mine[0, half:, :], got[0, half:, :])
    down_now[...] = plus(mine[1, :half, :], got[1, :half, :])
    down_late[...] = plus(mine[1, half:, :], got[1, half:, :])


def add_body(a, b, c, d, first, second):
    first[...] = plus(a[...], b[...])
    second[...] = plus(c[...], d[...])


def finish_body(mine, got, up_late, up_now, down_now, down_late, *outs):
    half = up_late.shape[0]
    add = lambda *values: functools.reduce(jnp.add, [v.astype(F32) for v in values])
    low = add(mine[:half, :], got[:half, :], up_late[...], down_now[...])
    high = add(mine[half:, :], got[half:, :], up_now[...], down_late[...])
    width = outs[0].shape[0]
    outs[0][...] = low[0:width]
    outs[1][0 : half - width, :] = low[width:]
    outs[1][half - width :, :] = high[0 : 2 * width - half]
    outs[2][...] = high[2 * width - half :]


def on_device(tokens, router, lists, slots, t_gate, t_up, t_down, e_gate, e_up, e_down):
    count, model = tokens.shape
    top = lists.shape[1]
    experts = router.shape[1]
    width = e_gate.shape[2]
    cap = 5 * count // experts
    rows = experts * STEP
    scale = top / math.sqrt(count * 256 * top / experts)
    cut = 48
    lists_t, slots_t = lists.T, slots.T
    shards = [t_gate.T, t_up.T, t_down]
    send, weights, shard = call(
        functools.partial(dispatch_body, cap),
        [shape((rows, model), BF16), shape((top, count), F32), shape((3 * cut, model), BF16)],
        [tokens, router.T, lists_t, slots_t] + shards,
        specs=[HBM] * 7,
        scratch=[
            pltpu.VMEM((count, model), BF16),
            pltpu.VMEM((experts, model), F32),
            pltpu.VMEM((top, count), jnp.int32),
            pltpu.VMEM((top, count), jnp.int32),
        ]
        + [pltpu.VMEM(t.shape, BF16) for t in shards]
        + [pltpu.VMEM((2 * count, model), BF16), pltpu.SemaphoreType.DMA((7,))],
        flops=2 * rows * 256 * model,
        grant=GRANT_D,
    )

    def shift(v, axis, size, by):
        return lax.ppermute(v, axis, [(s, (s + by) % size) for s in range(size)])

    pair = shift(shard, "zp", 2, 1)
    after = shift(shard, "y", 4, 1)
    before = shift(shard, "y", 4, -1)
    pair_after = shift(pair, "y", 4, 1)
    pair_before = shift(pair, "y", 4, -1)
    far = shift(after, "y", 4, 1)
    pair_far = shift(pair_before, "y", 4, -1)
    gathered = jnp.stack([shard, pair, after, before, pair_after, pair_before], axis=0)
    gathered_far = jnp.stack([far, pair_far], axis=0)

    def exchange(v):
        v = v.reshape(experts, -1, v.shape[1])
        out = lax.all_to_all(v, EXPERT, 0, 0, tiled=True)
        return out.reshape(-1, v.shape[2])

    recv = exchange(send)
    gate_t, up_t, down = e_gate[0].T, e_up[0].T, e_down[0]
    weight_buf = pltpu.VMEM((width, model), BF16)
    swap = [(0, 1), (1, 0)]
    other = lax.ppermute(gathered, "core", swap)
    other_far = lax.ppermute(gathered_far, "core", swap)
    x, slope, act, hidden, ret = call(
        functools.partial(forward_body, cap),
        [shape((rows, model), BF16), shape((width, rows), F32), shape((width, rows), F32)]
        + [shape((width, rows), BF16), shape((2 * experts * cap, model // 2), BF16)],
        [recv, gate_t, up_t, down, gathered, gathered_far, other, other_far],
        specs=[VMEM] * 3 + [HBM] * 5,
        out_specs=[HBM, HBM, HBM, HBM, VMEM],
        scratch=[
            weight_buf,
            pltpu.VMEM((16,) + shard.shape, BF16),
            pltpu.VMEM((rows, model), BF16),
            pltpu.VMEM((width, rows), F32),
            pltpu.VMEM((width, rows), F32),
            pltpu.VMEM((width, rows), BF16),
            pltpu.SemaphoreType.DMA((9,)),
        ],
        flops=6 * rows * (width + 768) * model,
        grant=GRANT_F,
    )
    index_buf = pltpu.VMEM((top, count), jnp.int32)
    (cot_send,) = call(
        functools.partial(error_body, cap, scale),
        [shape((2 * experts * cap, model // 2), BF16)],
        [exchange(ret), weights, lists_t, slots_t],
        specs=[VMEM, VMEM, HBM, HBM],
        scratch=[index_buf] * 2 + [pltpu.SemaphoreType.DMA((2,))],
        flops=2 * rows * 512 * model,
    )
    tall = 3 * width
    side = shape((width, rows), BF16)
    one, two = shape((tall, 128), BF16), shape((2, tall, 128), BF16)
    d_gate, d_up, cot, far_mine, far_theirs = call(
        functools.partial(grad_body, cap),
        [side] * 2 + [shape((rows, model), BF16)] + [one] * 2,
        [exchange(cot_send), x, slope, act, hidden, down],
        flops=4 * rows * width * model,
        grant=GRANT_G,
    )
    far_got = lax.ppermute(far_theirs, "core", swap)
    parts = [d_gate, d_up, hidden, x, cot]
    mine, theirs = call(near_body, [two] * 2, parts, flops=3 * rows * width * model, grant=GRANT_G)
    got = lax.ppermute(theirs, "core", swap)
    half = tall // 2
    halves = shape((half, 128), BF16)
    up = [(s, (s + 1) % 4) for s in range(4)]
    dn = [(s, (s - 1) % 4) for s in range(4)]
    far_up, far_down = call(far_body, [halves] * 2, [far_mine, far_got])
    a = lax.ppermute(far_up, "x", up)
    b = lax.ppermute(far_down, "x", dn)
    up_late, up_now, down_now, down_late = call(fold_body, [halves] * 4, [mine, got])
    now_up = lax.ppermute(up_now, "x", up)
    now_dn = lax.ppermute(down_now, "x", dn)
    own_mine, own_theirs = call(
        own_body, [one] * 2, parts, flops=3 * rows * width * model // 2, grant=GRANT_G
    )
    own_got = lax.ppermute(own_theirs, "core", swap)
    late_up, late_dn = call(add_body, [halves] * 2, [up_late, a, down_late, b])
    late_up = lax.ppermute(late_up, "x", up)
    late_dn = lax.ppermute(late_dn, "x", dn)
    g, u, d = call(
        finish_body,
        [shape((width, 128), F32)] * 3,
        [own_mine, own_got, late_up, now_up, now_dn, late_dn],
    )
    return g.T[None], u.T[None], d[None]


def solution(mesh):
    fine = Mesh(mesh.devices.reshape(4, 2, 4, 2, 4), ALL)

    return jax.shard_map(
        on_device,
        mesh=fine,
        in_specs=(
            P(ALL, None),
            P(),
            P(ALL, None),
            P(ALL, None),
            P(None, EXPERT),
            P(None, EXPERT),
            P(EXPERT, None),
            P(EXPERT, None, None),
            P(EXPERT, None, None),
            P(EXPERT, None, None),
        ),
        out_specs=(P(EXPERT, DP, None), P(EXPERT, DP, None), P(EXPERT, None, DP)),
        check_vma=False,
    )
```

```python
import functools
import math

import jax
import jax.numpy as jnp
from jax import lax
from jax.experimental import pallas as pl
from jax.experimental.pallas import tpu as pltpu
from jax.sharding import Mesh, PartitionSpec as P


BF16 = jnp.bfloat16
F32 = jnp.float32
ALL = ("x", "core", "zq", "zp", "y")
DP = ("x", "core")
EXPERT = ("zq", "zp", "y")
VMEM = pl.BlockSpec(memory_space=pltpu.VMEM)
HBM = pl.BlockSpec(memory_space=pltpu.MemorySpace.HBM)
GRANT_D, GRANT_F, GRANT_G = 62, 49, 24
STEP = 24


def call(body, outs, args, specs=None, out_specs=None, scratch=(), flops=0, grant=24):
    moved = sum(a.size * a.dtype.itemsize for a in args)
    moved += sum(math.prod(o.shape) * o.dtype.itemsize for o in outs)
    return pl.pallas_call(
        body,
        out_shape=tuple(outs),
        in_specs=specs or [VMEM] * len(args),
        out_specs=tuple(out_specs or [VMEM] * len(outs)),
        scratch_shapes=list(scratch),
        cost_estimate=pl.CostEstimate(flops=flops, bytes_accessed=moved, transcendentals=0),
        compiler_params=pltpu.CompilerParams(vmem_limit_bytes=grant * 1024 * 1024),
    )(*args)


def shape(dims, dtype):
    return jax.ShapeDtypeStruct(dims, dtype)


def nt(a, b):
    return lax.dot_general(a, b, (((1,), (1,)), ((), ())), preferred_element_type=F32)


def tn(a, b):
    return lax.dot_general(a, b, (((0,), (0,)), ((), ())), preferred_element_type=F32)


def nn(a, b):
    return jnp.dot(a, b, preferred_element_type=F32)


def sigmoid(v):
    return 1.0 / (1.0 + jnp.exp(-v))


def split(v):
    high = v.astype(BF16)
    return high, (v - high.astype(F32)).astype(BF16)


def as_bf16(mask):
    return jnp.where(mask, 1.0, 0.0).astype(BF16)


def iota(dims, axis):
    return lax.broadcasted_iota(jnp.int32, dims, axis)


def fetch(pairs, sems):
    copies = [pltpu.make_async_copy(src, dst, sems.at[i]) for i, (src, dst) in enumerate(pairs)]
    for copy in copies:
        copy.start()
    return copies


def quotient(v, by):
    return ((v.astype(F32) + 0.5) * (1.0 / by)).astype(jnp.int32)


def dispatch_body(
    cap, tok_h, router_h, lists_h, slots_h, gate_h, up_h, down_h, send, weights, shard,
    tok, router, lists, slots, gate, up, down, ext, sems,
):
    copies = fetch(
        [(router_h, router), (tok_h, tok), (lists_h, lists), (slots_h, slots)]
        + [(gate_h, gate), (up_h, up), (down_h, down)],
        sems,
    )
    for copy in copies[:4]:
        copy.wait()
    experts, count = router.shape[0], tok.shape[0]
    top = lists.shape[0]
    rows = experts * STEP
    logits = lax.dot_general(
        router[...],
        tok[...].astype(F32),
        (((1,), (1,)), ((), ())),
        precision=lax.Precision.HIGHEST,
        preferred_element_type=F32,
    )
    which = iota((experts, count), 0)
    picked = [
        jnp.sum(jnp.where(which == lists[k : k + 1, :], logits, 0.0), axis=0, keepdims=True)
        for k in range(top)
    ]
    gates = [sigmoid(p) for p in picked]
    total = functools.reduce(jnp.add, gates)
    parts = [g / total for g in gates]
    for k in range(top):
        weights[k : k + 1, :] = parts[k]
    spread = jnp.concatenate(
        [jnp.where(which == lists[k : k + 1, :], parts[k], 0.0) for k in range(top)], axis=1
    )
    high, low = split(spread)
    slot = iota((128, count), 0)
    place = jnp.concatenate([as_bf16(slot == slots[k : k + 1, :]) for k in range(top)], axis=1)
    ext[0:count, :] = tok[...]
    ext[count:, :] = jnp.zeros((ext.shape[0] - count, ext.shape[1]), BF16)
    ext[count : count + experts, 0:128] = nt(high, place).astype(BF16)
    ext[count : count + experts, 128:256] = nt(low, place).astype(BF16)
    row = iota((rows, count), 0)
    hit = functools.reduce(
        jnp.logical_or,
        [row == lists[k : k + 1, :] * STEP + slots[k : k + 1, :] for k in range(top)],
    )
    extra = row == iota((rows, count), 1) * STEP + cap
    onehot = jnp.concatenate([as_bf16(hit), as_bf16(extra)], axis=1)
    send[...] = nn(onehot, ext[...]).astype(BF16)
    for copy in copies[4:]:
        copy.wait()
    core = lax.axis_index("core")
    cut = shard.shape[0] // 3
    for i, piece in enumerate((gate, up, down)):
        units = piece.shape[0]
        at = i * cut
        full = (units - cut) // 16 * 16

        @pl.when(core == 0)
        def _(piece=piece, at=at):
            shard[at : at + cut, :] = piece[0:cut, :]

        @pl.when(core != 0)
        def _(piece=piece, at=at, full=full, units=units):
            shard[at : at + full, :] = piece[cut : cut + full, :]
            shard[at + full : at + cut, :] = jnp.zeros((cut - full, shard.shape[1]), BF16)
            shard[at + full : at + units - cut, :] = piece[cut + full : units, :]


def packing(cap, flip):
    dims = (8 * STEP, 8 * cap) if flip else (8 * cap, 8 * STEP)
    wire, wide = iota(dims, 1 if flip else 0), iota(dims, 0 if flip else 1)
    part = quotient(wire, cap)
    block = quotient(wire, 2 * cap)
    half = part - 2 * block
    return as_bf16(wide == half * (4 * STEP) + block * STEP + wire - part * cap)


def forward_body(
    cap, recv, gate, up_h, down_h, own_h, own_far_h, other_h, other_far_h, rows, slope, act, middle,
    ret, up, down, piece, x_out, slope_out, act_out, middle_out, sems,
):
    pairs, first_unit = [(up_h, up), (down_h, down)], 0
    for source in (own_h, own_far_h, other_h, other_far_h):
        pairs.append((source, piece.at[first_unit : first_unit + source.shape[0]]))
        first_unit += source.shape[0]
    copies = fetch(pairs, sems)
    count, model = recv.shape

    def save(src, dst, at):
        copy = pltpu.make_async_copy(src, dst, sems.at[at])
        copy.start()
        return copy

    experts = count // STEP
    line = iota((count, 128), 0)
    slot = line - quotient(line, STEP) * STEP
    keep = as_bf16(slot < cap)
    x = recv[...] * jnp.concatenate([keep] * (model // 128), axis=1)
    x_out[...] = x
    saves = [save(x_out, rows, 6)]
    pick = as_bf16(iota((experts, count), 1) == iota((experts, count), 0) * STEP + cap)
    found = nn(pick, recv[:, 0:256]).astype(BF16)
    row = iota((count, experts), 0)
    first = iota((count, experts), 1) * STEP
    spread = as_bf16(jnp.logical_and(row >= first, row < first + STEP))
    wide = nn(spread, found)
    wide = wide[:, 0:128] + wide[:, 128:256]
    mine = jnp.logical_and(iota((count, 128), 1) == slot, slot < cap)
    weight = jnp.sum(jnp.where(mine, wide, 0.0), axis=1, keepdims=True)
    g = nt(gate[...], x)
    copies[0].wait()
    u = nt(up[...], x)
    s = sigmoid(g)
    a = g * s
    act_out[...] = a
    saves.append(save(act_out, act, 7))
    slope_out[...] = u * s * (1.0 + g * (1.0 - s))
    saves.append(save(slope_out, slope, 8))
    hidden = (a * u).astype(BF16)
    middle_out[...] = hidden
    saves.append(save(middle_out, middle, 9))
    copies[1].wait()
    acc = weight * tn(hidden, down[...])
    units = piece.shape[1] // 3
    take = lambda i: piece[:, i * units : (i + 1) * units, :].reshape(-1, model)
    for copy in copies[2:]:
        copy.wait()
    a = nt(take(0), x)
    b = nt(take(1), x)
    hidden = (a * sigmoid(a) * b).astype(BF16)
    acc = acc - tn(hidden, take(2))
    result = acc.astype(BF16)
    pack = packing(cap, False)
    tall = 4 * STEP
    for i in range(experts // 4):
        part = result[i * tall : (i + 1) * tall, :]
        both = jnp.concatenate([part[:, : model // 2], part[:, model // 2 :]], axis=0)
        ret[i * 8 * cap : (i + 1) * 8 * cap, :] = nn(pack, both).astype(BF16)
    for copy in saves:
        copy.wait()


def error_body(cap, scale, ret, weights, lists_h, slots_h, send, lists, slots, sems):
    copies = fetch([(lists_h, lists), (slots_h, slots)], sems)
    top, count = lists.shape
    rows, half_width = ret.shape
    row = iota((rows, count), 0)
    part = quotient(row, cap)
    half = jnp.bitwise_and(part, 1)
    key = row - cap * half
    left = half == 0
    for copy in copies:
        copy.wait()
    hits = [key == lists[k : k + 1, :] * (2 * cap) + slots[k : k + 1, :] for k in range(top)]
    hit = functools.reduce(jnp.logical_or, hits)
    value = ret[...]
    error = scale * jnp.concatenate(
        [
            tn(as_bf16(jnp.logical_and(hit, left)), value),
            tn(as_bf16(jnp.logical_and(hit, jnp.logical_not(left))), value),
        ],
        axis=1,
    )
    high, low = split(error)
    spread = functools.reduce(
        jnp.add, [jnp.where(hits[k], weights[k : k + 1, :], 0.0) for k in range(top)]
    )
    w_high, w_low = split(spread)
    lhs = jnp.concatenate([w_high, w_high, w_low], axis=1)
    rhs = jnp.concatenate([high, low, high], axis=0)
    side = jnp.concatenate([left] * (half_width // count), axis=1)
    send[...] = jnp.where(
        side, nn(lhs, rhs[:, :half_width]), nn(lhs, rhs[:, half_width:])
    ).astype(BF16)


def chunk(parts, rows, cot, rels, puts):
    core, x_at = lax.axis_index("core"), lax.axis_index("x")

    def columns(ref):
        pieces = []
        for rel in rels:
            first = pl.multiple_of(jnp.bitwise_and(x_at + rel, 3) * 256, 256)
            pieces.append(ref[:, pl.ds(first, 256)])
        return jnp.concatenate(pieces, axis=1)

    side = columns(rows)
    width = parts[0].shape[0]
    for i, part in enumerate(parts):
        value = nn(part, columns(cot) if i == 2 else side).astype(BF16)
        at = slice(i * width, (i + 1) * width)
        for j, (mine, theirs) in enumerate(puts):
            left = value[:, j * 256 : j * 256 + 128]
            right = value[:, j * 256 + 128 : (j + 1) * 256]

            @pl.when(core == 0)
            def _(left=left, right=right, at=at, mine=mine, theirs=theirs):
                mine(at, left)
                theirs(at, right)

            @pl.when(core != 0)
            def _(left=left, right=right, at=at, mine=mine, theirs=theirs):
                mine(at, right)
                theirs(at, left)


def putter(ref, at=None):
    def put(rows, value):
        if at is None:
            ref[rows, :] = value
        else:
            ref[at, rows, :] = value

    return put


def grad_body(cap, wire, rows, slope, act, hidden, down, d_gate, d_up, cot, mine, theirs):
    count, model = cot.shape
    unpack = packing(cap, True)
    tall = 4 * STEP
    for i in range(count // tall):
        both = nn(unpack, wire[i * 8 * cap : (i + 1) * 8 * cap, :]).astype(BF16)
        cot[i * tall : (i + 1) * tall, : model // 2] = both[:tall]
        cot[i * tall : (i + 1) * tall, model // 2 :] = both[tall:]
    grad_hidden = nt(down[...], cot[...])
    d_gate[...] = (grad_hidden * slope[...]).astype(BF16)
    d_up[...] = (grad_hidden * act[...]).astype(BF16)
    parts = (d_gate[...], d_up[...], hidden[...])
    chunk(parts, rows, cot, (2,), [(putter(mine), putter(theirs))])


def near_body(d_gate, d_up, hidden, rows, cot, mine, theirs):
    parts = (d_gate[...], d_up[...], hidden[...])
    puts = [(putter(mine, at), putter(theirs, at)) for at in range(2)]
    chunk(parts, rows, cot, (1, 3), puts)


def own_body(d_gate, d_up, hidden, rows, cot, mine, theirs):
    parts = (d_gate[...], d_up[...], hidden[...])
    chunk(parts, rows, cot, (0,), [(putter(mine), putter(theirs))])


def plus(a, b):
    return (a.astype(F32) + b.astype(F32)).astype(BF16)


def far_body(mine, got, up, down):
    half = up.shape[0]
    up[...] = plus(mine[:half, :], got[:half, :])
    down[...] = plus(mine[half:, :], got[half:, :])


def fold_body(mine, got, up_late, up_now, down_now, down_late):
    half = up_late.shape[0]
    up_late[...] = plus(mine[0, :half, :], got[0, :half, :])
    up_now[...] = plus(mine[0, half:, :], got[0, half:, :])
    down_now[...] = plus(mine[1, :half, :], got[1, :half, :])
    down_late[...] = plus(mine[1, half:, :], got[1, half:, :])


def add_body(a, b, c, d, first, second):
    first[...] = plus(a[...], b[...])
    second[...] = plus(c[...], d[...])


def finish_body(mine, got, up_late, up_now, down_now, down_late, *outs):
    half = up_late.shape[0]
    add = lambda *values: functools.reduce(jnp.add, [v.astype(F32) for v in values])
    low = add(mine[:half, :], got[:half, :], up_late[...], down_now[...])
    high = add(mine[half:, :], got[half:, :], up_now[...], down_late[...])
    width = outs[0].shape[0]
    outs[0][...] = low[0:width]
    outs[1][0 : half - width, :] = low[width:]
    outs[1][half - width :, :] = high[0 : 2 * width - half]
    outs[2][...] = high[2 * width - half :]


def on_device(tokens, router, lists, slots, t_gate, t_up, t_down, e_gate, e_up, e_down):
    count, model = tokens.shape
    top = lists.shape[1]
    experts = router.shape[1]
    width = e_gate.shape[2]
    cap = 5 * count // experts
    rows = experts * STEP
    scale = top / math.sqrt(count * 256 * top / experts)
    cut = 48
    lists_t, slots_t = lists.T, slots.T
    shards = [t_gate.T, t_up.T, t_down]
    send, weights, shard = call(
        functools.partial(dispatch_body, cap),
        [shape((rows, model), BF16), shape((top, count), F32), shape((3 * cut, model), BF16)],
        [tokens, router.T, lists_t, slots_t] + shards,
        specs=[HBM] * 7,
        scratch=[
            pltpu.VMEM((count, model), BF16),
            pltpu.VMEM((experts, model), F32),
            pltpu.VMEM((top, count), jnp.int32),
            pltpu.VMEM((top, count), jnp.int32),
        ]
        + [pltpu.VMEM(t.shape, BF16) for t in shards]
        + [pltpu.VMEM((2 * count, model), BF16), pltpu.SemaphoreType.DMA((7,))],
        flops=2 * rows * 256 * model,
        grant=GRANT_D,
    )

    def shift(v, axis, size, by):
        return lax.ppermute(v, axis, [(s, (s + by) % size) for s in range(size)])

    pair = shift(shard, "zp", 2, 1)
    after = shift(shard, "y", 4, 1)
    before = shift(shard, "y", 4, -1)
    pair_after = shift(pair, "y", 4, 1)
    pair_before = shift(pair, "y", 4, -1)
    far = shift(after, "y", 4, 1)
    pair_far = shift(pair_before, "y", 4, -1)
    gathered = jnp.stack([shard, pair, after, before, pair_after, pair_before], axis=0)
    gathered_far = jnp.stack([far, pair_far], axis=0)

    def exchange(v):
        v = v.reshape(experts, -1, v.shape[1])
        out = lax.all_to_all(v, EXPERT, 0, 0, tiled=True)
        return out.reshape(-1, v.shape[2])

    recv = exchange(send)
    gate_t, up_t, down = e_gate[0].T, e_up[0].T, e_down[0]
    weight_buf = pltpu.VMEM((width, model), BF16)
    swap = [(0, 1), (1, 0)]
    other = lax.ppermute(gathered, "core", swap)
    other_far = lax.ppermute(gathered_far, "core", swap)
    x, slope, act, hidden, ret = call(
        functools.partial(forward_body, cap),
        [shape((rows, model), BF16), shape((width, rows), F32), shape((width, rows), F32)]
        + [shape((width, rows), BF16), shape((2 * experts * cap, model // 2), BF16)],
        [recv, gate_t, up_t, down, gathered, gathered_far, other, other_far],
        specs=[VMEM] * 2 + [HBM] * 6,
        out_specs=[HBM, HBM, HBM, HBM, VMEM],
        scratch=[
            weight_buf,
            weight_buf,
            pltpu.VMEM((16,) + shard.shape, BF16),
            pltpu.VMEM((rows, model), BF16),
            pltpu.VMEM((width, rows), F32),
            pltpu.VMEM((width, rows), F32),
            pltpu.VMEM((width, rows), BF16),
            pltpu.SemaphoreType.DMA((10,)),
        ],
        flops=6 * rows * (width + 768) * model,
        grant=GRANT_F,
    )
    index_buf = pltpu.VMEM((top, count), jnp.int32)
    (cot_send,) = call(
        functools.partial(error_body, cap, scale),
        [shape((2 * experts * cap, model // 2), BF16)],
        [exchange(ret), weights, lists_t, slots_t],
        specs=[VMEM, VMEM, HBM, HBM],
        scratch=[index_buf] * 2 + [pltpu.SemaphoreType.DMA((2,))],
        flops=2 * rows * 512 * model,
    )
    tall = 3 * width
    side = shape((width, rows), BF16)
    one, two = shape((tall, 128), BF16), shape((2, tall, 128), BF16)
    d_gate, d_up, cot, far_mine, far_theirs = call(
        functools.partial(grad_body, cap),
        [side] * 2 + [shape((rows, model), BF16)] + [one] * 2,
        [exchange(cot_send), x, slope, act, hidden, down],
        flops=4 * rows * width * model,
        grant=GRANT_G,
    )
    far_got = lax.ppermute(far_theirs, "core", swap)
    parts = [d_gate, d_up, hidden, x, cot]
    mine, theirs = call(near_body, [two] * 2, parts, flops=3 * rows * width * model, grant=GRANT_G)
    got = lax.ppermute(theirs, "core", swap)
    half = tall // 2
    halves = shape((half, 128), BF16)
    up = [(s, (s + 1) % 4) for s in range(4)]
    dn = [(s, (s - 1) % 4) for s in range(4)]
    far_up, far_down = call(far_body, [halves] * 2, [far_mine, far_got])
    a = lax.ppermute(far_up, "x", up)
    b = lax.ppermute(far_down, "x", dn)
    up_late, up_now, down_now, down_late = call(fold_body, [halves] * 4, [mine, got])
    now_up = lax.ppermute(up_now, "x", up)
    now_dn = lax.ppermute(down_now, "x", dn)
    own_mine, own_theirs = call(
        own_body, [one] * 2, parts, flops=3 * rows * width * model // 2, grant=GRANT_G
    )
    own_got = lax.ppermute(own_theirs, "core", swap)
    late_up, late_dn = call(add_body, [halves] * 2, [up_late, a, down_late, b])
    late_up = lax.ppermute(late_up, "x", up)
    late_dn = lax.ppermute(late_dn, "x", dn)
    g, u, d = call(
        finish_body,
        [shape((width, 128), F32)] * 3,
        [own_mine, own_got, late_up, now_up, now_dn, late_dn],
    )
    return g.T[None], u.T[None], d[None]


def solution(mesh):
    fine = Mesh(mesh.devices.reshape(4, 2, 4, 2, 4), ALL)

    return jax.shard_map(
        on_device,
        mesh=fine,
        in_specs=(
            P(ALL, None),
            P(),
            P(ALL, None),
            P(ALL, None),
            P(None, EXPERT),
            P(None, EXPERT),
            P(EXPERT, None),
            P(EXPERT, None, None),
            P(EXPERT, None, None),
            P(EXPERT, None, None),
        ),
        out_specs=(P(EXPERT, DP, None), P(EXPERT, DP, None), P(EXPERT, None, DP)),
        check_vma=False,
    )
```
